32 devices in a mesh: outer: 4 (over y, core), row: 4 (over z), col: 2 (over x).
Axes of the slice: x: 2, y: 2, z: 4, core: 2. Of those that a mesh axis runs over, the one named last changes fastest.
Arguments:
- activations: bfloat16 [2048, 9216], P(('outer', 'col'), 'row'), may hold values from -13 to 13
- out_grads: bfloat16 [2048, 8192], P(('outer', 'row'), 'col'), may hold values from -13 to 13
- row_moment: float32 [9216], P(('row', 'outer')), may hold values from 0.3 to 3
- col_moment: float32 [8192], P('col'), may hold values from 0.3 to 3
Outputs:
- update: bfloat16 [9216, 8192], P(('row', 'outer'), 'col')
- new_row: float32 [9216], P(('row', 'outer'))
- new_col: float32 [8192], P('col')
The draws below stay inside these ranges and needn't reach their ends.
All inputs are finite; a program needn't handle non-finite values.
Results may differ from the reference program's by a relative error of at most 0.001.
Values may be sent and summed in bfloat16 or wider, within the bound.
A program may use at most 128 MiB of HBM per device.

```python
import math
import jax
import jax.numpy as jnp
from jax import lax

D = 9216
F = 8192
STEP = 2
TOKENS = 2048


def scaled_block(key, count, width):
    first, second = jax.random.split(key)
    position = jnp.arange(width, dtype=jnp.float32) / max(width - 1, 1)
    rough = 10.0 ** jax.random.uniform(second, (width,), jnp.float32, -0.25, 0.25)
    base = jax.random.truncated_normal(first, -4.0, 4.0, (count, width), jnp.float32)
    rising = jnp.sqrt((1.0 + 2.0 * position) / 3.0) * 1.7320508
    return (base * (rough * rising)[None, :]).astype(jnp.bfloat16)


def draw_activations(key, part):
    return scaled_block(jax.random.fold_in(key, 11), TOKENS, D)


def draw_out_grads(key, part):
    return scaled_block(jax.random.fold_in(key, 23), TOKENS, F)


def block_scale(key, dims, pieces, least, high):
    def one(axis_at, shards_of):
        draws = jax.random.uniform(jax.random.fold_in(jax.random.fold_in(key, 6), axis_at), (shards_of,), jnp.float32, least / len(pieces), high / len(pieces))
        return jnp.repeat(jnp.exp(draws), dims[axis_at] // shards_of).reshape((-1,) + (1,) * (len(dims) - axis_at - 1))

    loudness = one(*pieces[0])
    for cut in pieces[1:]:
        loudness = loudness * one(*cut)
    return loudness


def setup_inputs(seed: int = 0) -> dict:
    arg_keys = jax.random.split(jax.random.key(seed), 5)
    activations = draw_activations(jax.random.fold_in(arg_keys[4], 71), 0)
    out_grads = draw_out_grads(jax.random.fold_in(arg_keys[4], 71), 0)
    row_moment = jnp.clip(jnp.exp(math.log(3.0) - 2.3025851 * jax.random.uniform(arg_keys[2], (D,), jnp.float32) ** block_scale(arg_keys[2], (D,), ((0, 16),), -0.2, 0.2)), 0.3, 3.0)
    col_moment = jnp.clip(jnp.exp(math.log(3.0) - 2.3025851 * jax.random.uniform(arg_keys[3], (F,), jnp.float32) ** block_scale(arg_keys[3], (F,), ((0, 2),), -0.2, 0.2)), 0.3, 3.0)
    return {"activations": activations, "out_grads": out_grads, "row_moment": row_moment, "col_moment": col_moment}


def reference(activations, out_grads, row_moment, col_moment):
    gradient = lax.dot_general(activations, out_grads, (((0,), (0,)), ((), ())), preferred_element_type=jnp.float32)
    gradient = gradient * (1.0 / TOKENS ** 0.5)
    squares = gradient * gradient
    row_squares = lax.optimization_barrier(jnp.sum(squares, axis=1))
    col_squares = lax.optimization_barrier(jnp.sum(squares, axis=0))
    decay_rate = 1.0 - STEP ** (-0.8)
    new_row = decay_rate * row_moment + (1.0 - decay_rate) * row_squares / F
    new_col = decay_rate * col_moment + (1.0 - decay_rate) * col_squares / D
    moment_total = jnp.sum(new_row)
    factor = lax.rsqrt(new_row[:, None] * new_col[None, :] * (D / moment_total))
    update = (gradient * factor).astype(jnp.bfloat16)
    return (update, new_row, new_col)
```

```python
import functools

import jax
import jax.numpy as jnp
from jax import lax
from jax.experimental import pallas as pl
from jax.experimental.pallas import tpu as pltpu
from jax.sharding import PartitionSpec as P

D = 9216
F = 8192
STEP = 2
MESH = pl.DeviceIdType.MESH
PIECES = 2


def kernel(
    nout, nz, ncol, scale, decay,
    a_ref, g_ref, rm_ref, cm_ref,
    grad_hbm, nr_ref, nc_ref, mt_ref,
    gs, av, acc, rowp, colbuf, colz, rowbuf, totz, toto,
    g_recv, zp_send, zm_send, y_send, p_send, a_recv, a1_send, a2_send, loc_sem, out_sem,
    c_send, c_recv, cz_send, cz_recv, r_send, r_recv, tz_send, tz_recv, to_send, to_recv,
):
    tg, width = g_ref.shape
    rows, ta = av.shape[1], av.shape[2]
    piece = width // PIECES
    o = lax.axis_index("outer")
    z = lax.axis_index("row")
    x = lax.axis_index("col")
    y, core = o // 2, o % 2
    oy = (1 - y) * 2 + core
    op = y * 2 + (1 - core)
    mate = z + 1 - 2 * (z % 2)

    def remote(src, dst, s, r, dev):
        return pltpu.make_async_remote_copy(
            src_ref=src, dst_ref=dst, send_sem=s, recv_sem=r, device_id=dev, device_id_type=MESH
        )

    barrier = pltpu.get_barrier_semaphore()
    for d in range(1, nout):
        pl.semaphore_signal(barrier, inc=1, device_id={"outer": (o + d) % nout}, device_id_type=MESH)
    for d in range(1, nz):
        pl.semaphore_signal(barrier, inc=1, device_id={"row": (z + d) % nz}, device_id_type=MESH)
    for d in range(1, ncol):
        pl.semaphore_signal(barrier, inc=1, device_id={"col": (x + d) % ncol}, device_id_type=MESH)
    pl.semaphore_wait(barrier, nout + nz + ncol - 3)

    def slot(oo, zz):
        return oo * nz + zz

    def place(s, h):
        return gs.at[pl.ds(pl.multiple_of(s * tg, tg), tg), pl.ds(h * piece, piece)]

    def g_copy(src, s, h, sem, dev):
        return remote(src, place(s, h), sem, g_recv.at[s, h], dev)

    def to_up(src, oo, zz, h):
        k = jnp.where(oo == o, zz, nz)
        return g_copy(src, slot(oo, zz), h, zp_send.at[k, h], {"row": jnp.minimum(z + 1, nz - 1)})

    def to_down(src, oo, zz, h):
        k = jnp.where(oo == o, zz, nz)
        return g_copy(src, slot(oo, zz), h, zm_send.at[k, h], {"row": jnp.maximum(z - 1, 0)})

    def to_y(src, zz, h):
        return g_copy(src, slot(o, zz), h, y_send.at[zz, h], {"outer": oy})

    def to_partner(src, oo, zz, h):
        k = jnp.where(oo == o, zz, nz + zz)
        return g_copy(src, slot(oo, zz), h, p_send.at[k, h], {"outer": op})

    def arrived(oo, zz, h):
        here = place(slot(oo, zz), h)
        to_partner(here, oo, zz, h).wait_recv()
        return here

    own = [g_ref.at[:, pl.ds(h * piece, piece)] for h in range(PIECES)]
    for h in range(PIECES):
        @pl.when(z < nz - 1)
        def _():
            to_up(own[h], o, z, h).start()

        @pl.when(z > 0)
        def _():
            to_down(own[h], o, z, h).start()

        to_y(own[h], z, h).start()
        to_partner(own[h], o, z, h).start()

    def a_first(d):
        target = (o + d) % nout
        return remote(a_ref.at[target], av.at[o * ncol + x], a1_send.at[d], a_recv.at[o * ncol + x], {"outer": target})

    def a_second(q, d):
        oo = (o + q) % nout
        k = oo * ncol + x
        src = a_ref.at[o] if q == 0 else av.at[k]
        return remote(src, av.at[k], a2_send.at[q, d], a_recv.at[k], {"col": (x + d) % ncol})

    for d in range(1, nout):
        a_first(d).start()
    for d in range(1, ncol):
        a_second(0, d).start()
    local_g = pltpu.make_async_copy(g_ref, gs.at[pl.ds(pl.multiple_of(slot(o, z) * tg, tg), tg), :], loc_sem.at[0])
    local_a = pltpu.make_async_copy(a_ref.at[o], av.at[o * ncol + x], loc_sem.at[1])
    local_g.start()
    local_a.start()

    def a_arrived(k):
        remote(av.at[k], av.at[k], a1_send.at[1], a_recv.at[k], {"outer": oy}).wait_recv()

    def y_arrived(zz, forward=False):
        for h in range(PIECES):
            here = arrived(oy, zz, h)
            to_partner(here, oy, zz, h).start()

    def extra(h, act):
        here = place(slot(oy, z), h)

        @pl.when(mate > z)
        def _():
            act(to_up(here, oy, z, h))

        @pl.when(mate < z)
        def _():
            act(to_down(here, oy, z, h))

    for s in range(1, nz):
        for h in range(PIECES):
            @pl.when(z - s >= 0)
            def _():
                here = arrived(o, z - s, h)

                @pl.when(z < nz - 1)
                def _():
                    to_up(here, o, z - s, h).start()

                @pl.when(z - s != mate)
                def _():
                    to_y(here, z - s, h).start()

                to_partner(here, o, z - s, h).start()

            @pl.when(z + s < nz)
            def _():
                here = arrived(o, z + s, h)

                @pl.when(z > 0)
                def _():
                    to_down(here, o, z + s, h).start()

                @pl.when(z + s != mate)
                def _():
                    to_y(here, z + s, h).start()

                to_partner(here, o, z + s, h).start()

        if s == 1:
            y_arrived(z)
            for q in range(1, nout):
                a_arrived(((o + q) % nout) * ncol + x)
                for d in range(1, ncol):
                    a_second(q, d).start()
        else:
            for zz in (z - (s - 1), z + (s - 1)):
                @pl.when((zz >= 0) & (zz < nz) & (zz != mate))
                def _():
                    y_arrived(zz)
        if s == max(nz - 2, 1):
            for h in range(PIECES):
                extra(h, lambda c: c.start())

    local_g.wait()
    local_a.wait()
    for d in range(1, ncol):
        for q in range(nout):
            a_arrived(((o + q) % nout) * ncol + (x + d) % ncol)
    for zz in range(nz):
        for h in range(PIECES):
            arrived(op, zz, h)
    tile = min(512, piece)
    per_piece = piece // tile

    def dots(yy, columns):
        total = None
        for k in range(2 * ncol):
            block = yy * 2 * ncol + k
            part = jnp.dot(
                av[block],
                gs[pl.ds(pl.multiple_of(block * ta, ta), ta), columns],
                preferred_element_type=jnp.float32,
            )
            total = part if total is None else total + part
        return total

    @pl.loop(0, width // tile)
    def _(j):
        columns = pl.ds(pl.multiple_of(j * tile, tile), tile)
        acc[:, columns] = dots(y, columns)

    rowp[...] = jnp.zeros_like(rowp)
    od = (1 - y) * 2 + (1 - core)
    for h in range(PIECES):
        for zz in (z - (nz - 1), z + (nz - 1)):
            @pl.when((zz >= 0) & (zz < nz) & (zz != mate))
            def _():
                here = arrived(oy, zz, h)
                to_partner(here, oy, zz, h).start()

        here = arrived(oy, mate, h)
        to_partner(here, oy, mate, h).start()
    for h in range(PIECES):
        for zz in range(nz):
            arrived(od, zz, h)

        @pl.loop(h * per_piece, (h + 1) * per_piece)
        def _(j):
            columns = pl.ds(pl.multiple_of(j * tile, tile), tile)
            grad = (acc[:, columns] + dots(1 - y, columns)) * scale
            acc[:, columns] = grad
            squares = grad * grad
            part = squares[:, :128]
            for i in range(1, tile // 128):
                part = part + squares[:, i * 128 : (i + 1) * 128]
            rowp[...] += part
            colbuf[0, :, columns] = jnp.sum(squares, axis=0, keepdims=True)

    out_copy = pltpu.make_async_copy(acc, grad_hbm, out_sem)
    out_copy.start()

    def c_first(d):
        return remote(colbuf.at[0], colbuf.at[nout - d], c_send.at[d], c_recv.at[nout - d], {"outer": (o + d) % nout})

    def c_second(d):
        return remote(colz.at[0], colz.at[nz - d], cz_send.at[d], cz_recv.at[nz - d], {"row": (z + d) % nz})

    def r_first(d):
        return remote(rowbuf.at[0], rowbuf.at[ncol - d], r_send.at[d], r_recv.at[ncol - d], {"col": (x + d) % ncol})

    def t_first(d):
        return remote(totz.at[0], totz.at[nz - d], tz_send.at[d], tz_recv.at[nz - d], {"row": (z + d) % nz})

    def t_second(d):
        return remote(toto.at[0], toto.at[nout - d], to_send.at[d], to_recv.at[nout - d], {"outer": (o + d) % nout})

    def finish(copies):
        for c in copies:
            c.wait()

    firsts = [c_first(d) for d in range(1, nout)]
    for c in firsts:
        c.start()
    rowbuf[0] = jnp.sum(jnp.transpose(rowp[...]), axis=0, keepdims=True)
    rights = [r_first(d) for d in range(1, ncol)]
    for c in rights:
        c.start()
    finish(rights)
    row_sq = rowbuf[0]
    for d in range(1, ncol):
        row_sq = row_sq + rowbuf[d]
    new_row = decay * rm_ref[...] + (1.0 - decay) * row_sq / F
    nr_ref[...] = new_row
    totz[0] = jnp.broadcast_to(jnp.sum(new_row, axis=1, keepdims=True), totz.shape[1:])
    tots = [t_first(d) for d in range(1, nz)]
    for c in tots:
        c.start()
    finish(firsts)
    col_sq = colbuf[0]
    for d in range(1, nout):
        col_sq = col_sq + colbuf[d]
    colz[0] = col_sq
    seconds = [c_second(d) for d in range(1, nz)]
    for c in seconds:
        c.start()
    finish(tots)
    total = totz[0]
    for d in range(1, nz):
        total = total + totz[d]
    toto[0] = total
    lasts = [t_second(d) for d in range(1, nout)]
    for c in lasts:
        c.start()
    finish(seconds)
    col_sq = colz[0]
    for d in range(1, nz):
        col_sq = col_sq + colz[d]
    nc_ref[...] = decay * cm_ref[...] + (1.0 - decay) * col_sq / D
    finish(lasts)
    total = toto[0]
    for d in range(1, nout):
        total = total + toto[d]
    mt_ref[...] = total

    for h in range(PIECES):
        for zz in range(nz):
            @pl.when((z < nz - 1) & (zz <= z))
            def _():
                to_up(place(slot(o, zz), h), o, zz, h).wait_send()

            @pl.when((z > 0) & (zz >= z))
            def _():
                to_down(place(slot(o, zz), h), o, zz, h).wait_send()

            @pl.when(zz != mate)
            def _():
                to_y(place(slot(o, zz), h), zz, h).wait_send()

            to_partner(place(slot(o, zz), h), o, zz, h).wait_send()
            to_partner(place(slot(oy, zz), h), oy, zz, h).wait_send()
        extra(h, lambda c: c.wait_send())
    for d in range(1, nout):
        a_first(d).wait_send()
    for q in range(nout):
        for d in range(1, ncol):
            a_second(q, d).wait_send()
    out_copy.wait()


def body(nout, nz, ncol, activations, out_grads, row_moment, col_moment):
    rows, width = row_moment.shape[0], col_moment.shape[0]
    ta, tg = activations.shape[0], out_grads.shape[0]
    tokens = ta * ncol * nout
    decay = 1.0 - STEP ** (-0.8)
    turned = activations.T.reshape(nout, rows, ta)
    f32, bf16 = jnp.float32, jnp.bfloat16
    vmem = pl.BlockSpec(memory_space=pltpu.VMEM)
    dma = pltpu.SemaphoreType.DMA
    grad, new_row, new_col, total = pl.pallas_call(
        functools.partial(kernel, nout, nz, ncol, 1.0 / tokens**0.5, decay),
        out_shape=(
            jax.ShapeDtypeStruct((rows, width), f32),
            jax.ShapeDtypeStruct((1, rows), f32),
            jax.ShapeDtypeStruct((1, width), f32),
            jax.ShapeDtypeStruct((1, 128), f32),
        ),
        in_specs=[vmem] * 4,
        out_specs=(pl.BlockSpec(memory_space=pl.ANY), vmem, vmem, vmem),
        scratch_shapes=[
            pltpu.VMEM((tokens, width), bf16),
            pltpu.VMEM((nout * ncol, rows, ta), bf16),
            pltpu.VMEM((rows, width), f32),
            pltpu.VMEM((rows, 128), f32),
            pltpu.VMEM((nout, 1, width), f32),
            pltpu.VMEM((nz, 1, width), f32),
            pltpu.VMEM((ncol, 1, rows), f32),
            pltpu.VMEM((nz, 1, 128), f32),
            pltpu.VMEM((nout, 1, 128), f32),
            dma((nout * nz, PIECES)),
            dma((nz + 1, PIECES)),
            dma((nz + 1, PIECES)),
            dma((nz, PIECES)),
            dma((2 * nz, PIECES)),
            dma((nout * ncol,)),
            dma((nout,)),
            dma((nout, ncol)),
            dma((2,)),
            dma,
            dma((nout,)), dma((nout,)),
            dma((nz,)), dma((nz,)),
            dma((ncol,)), dma((ncol,)),
            dma((nz,)), dma((nz,)),
            dma((nout,)), dma((nout,)),
        ],
        compiler_params=pltpu.CompilerParams(
            collective_id=0, has_side_effects=True, vmem_limit_bytes=56 * 1024 * 1024
        ),
    )(turned, out_grads, row_moment.reshape(1, rows), col_moment.reshape(1, width))
    factor = lax.rsqrt(new_row.reshape(rows)[:, None] * new_col * (D / total[0, 0]))
    update = (grad * factor).astype(bf16)
    return (update, new_row.reshape(rows), new_col.reshape(width))


def solution(mesh):
    nout, nz, ncol = mesh.shape["outer"], mesh.shape["row"], mesh.shape["col"]
    return jax.shard_map(
        functools.partial(body, nout, nz, ncol),
        mesh=mesh,
        in_specs=(
            P(("outer", "col"), "row"),
            P(("outer", "row"), "col"),
            P(("row", "outer")),
            P("col"),
        ),
        out_specs=(P(("row", "outer"), "col"), P(("row", "outer")), P("col")),
        check_vma=False,
    )
```

```python
import functools

import jax
import jax.numpy as jnp
from jax import lax
from jax.experimental import pallas as pl
from jax.experimental.pallas import tpu as pltpu
from jax.sharding import PartitionSpec as P

D = 9216
F = 8192
STEP = 2
MESH = pl.DeviceIdType.MESH
PIECES = 4
BY_Y = 1


def kernel(
    nout, nz, ncol, scale, decay,
    a_ref, g_ref, rm_ref, cm_ref,
    grad_hbm, nr_ref, nc_ref, mt_ref,
    gs, av, acc, rowp, colbuf, colz, rowbuf, totz, toto,
    g_recv, zp_send, zm_send, y_send, p_send, a_recv, a1_send, a2_send, loc_sem, out_sem,
    c_send, c_recv, cz_send, cz_recv, r_send, r_recv, tz_send, tz_recv, to_send, to_recv,
):
    tg, width = g_ref.shape
    rows, ta = av.shape[1], av.shape[2]
    piece = width // PIECES
    o = lax.axis_index("outer")
    z = lax.axis_index("row")
    x = lax.axis_index("col")
    y, core = o // 2, o % 2
    oy = (1 - y) * 2 + core
    op = y * 2 + (1 - core)
    mate = z + 1 - 2 * (z % 2)

    def remote(src, dst, s, r, dev):
        return pltpu.make_async_remote_copy(
            src_ref=src, dst_ref=dst, send_sem=s, recv_sem=r, device_id=dev, device_id_type=MESH
        )

    barrier = pltpu.get_barrier_semaphore()
    for d in range(1, nout):
        pl.semaphore_signal(barrier, inc=1, device_id={"outer": (o + d) % nout}, device_id_type=MESH)
    for d in range(1, nz):
        pl.semaphore_signal(barrier, inc=1, device_id={"row": (z + d) % nz}, device_id_type=MESH)
    for d in range(1, ncol):
        pl.semaphore_signal(barrier, inc=1, device_id={"col": (x + d) % ncol}, device_id_type=MESH)
    pl.semaphore_wait(barrier, nout + nz + ncol - 3)

    def slot(oo, zz):
        return oo * nz + zz

    def place(s, h):
        return gs.at[pl.ds(pl.multiple_of(s * tg, tg), tg), pl.ds(h * piece, piece)]

    def g_copy(src, s, h, sem, dev):
        return remote(src, place(s, h), sem, g_recv.at[s, h], dev)

    def to_up(src, oo, zz, h):
        k = jnp.where(oo == o, zz, nz)
        return g_copy(src, slot(oo, zz), h, zp_send.at[k, h], {"row": jnp.minimum(z + 1, nz - 1)})

    def to_down(src, oo, zz, h):
        k = jnp.where(oo == o, zz, nz)
        return g_copy(src, slot(oo, zz), h, zm_send.at[k, h], {"row": jnp.maximum(z - 1, 0)})

    def to_y(src, zz, h):
        return g_copy(src, slot(o, zz), h, y_send.at[zz, h], {"outer": oy})

    def to_partner(src, oo, zz, h):
        k = jnp.where(oo == o, zz, nz + zz)
        return g_copy(src, slot(oo, zz), h, p_send.at[k, h], {"outer": op})

    def arrived(oo, zz, h):
        here = place(slot(oo, zz), h)
        to_partner(here, oo, zz, h).wait_recv()
        return here

    own = [g_ref.at[:, pl.ds(h * piece, piece)] for h in range(PIECES)]
    for h in range(PIECES):
        @pl.when(z < nz - 1)
        def _():
            to_up(own[h], o, z, h).start()

        @pl.when(z > 0)
        def _():
            to_down(own[h], o, z, h).start()

        to_y(own[h], z, h).start()
        to_partner(own[h], o, z, h).start()

    def a_first(d):
        target = (o + d) % nout
        return remote(a_ref.at[target], av.at[o * ncol + x], a1_send.at[d], a_recv.at[o * ncol + x], {"outer": target})

    def a_second(q, d):
        oo = (o + q) % nout
        k = oo * ncol + x
        src = a_ref.at[o] if q == 0 else av.at[k]
        return remote(src, av.at[k], a2_send.at[q, d], a_recv.at[k], {"col": (x + d) % ncol})

    for d in range(1, nout):
        a_first(d).start()
    for d in range(1, ncol):
        a_second(0, d).start()
    local_g = pltpu.make_async_copy(g_ref, gs.at[pl.ds(pl.multiple_of(slot(o, z) * tg, tg), tg), :], loc_sem.at[0])
    local_a = pltpu.make_async_copy(a_ref.at[o], av.at[o * ncol + x], loc_sem.at[1])
    local_g.start()
    local_a.start()

    def a_arrived(k):
        remote(av.at[k], av.at[k], a1_send.at[1], a_recv.at[k], {"outer": oy}).wait_recv()

    def y_arrived(zz, forward=False):
        for h in range(PIECES):
            here = arrived(oy, zz, h)
            to_partner(here, oy, zz, h).start()

    def extra(h, act):
        here = place(slot(oy, z), h)

        @pl.when(mate > z)
        def _():
            act(to_up(here, oy, z, h))

        @pl.when(mate < z)
        def _():
            act(to_down(here, oy, z, h))

    for s in range(1, nz):
        for h in range(PIECES):
            @pl.when(z - s >= 0)
            def _():
                here = arrived(o, z - s, h)

                @pl.when(z < nz - 1)
                def _():
                    to_up(here, o, z - s, h).start()

                @pl.when((z - s != mate) | (h < BY_Y))
                def _():
                    to_y(here, z - s, h).start()

                to_partner(here, o, z - s, h).start()

            @pl.when(z + s < nz)
            def _():
                here = arrived(o, z + s, h)

                @pl.when(z > 0)
                def _():
                    to_down(here, o, z + s, h).start()

                @pl.when((z + s != mate) | (h < BY_Y))
                def _():
                    to_y(here, z + s, h).start()

                to_partner(here, o, z + s, h).start()

        if s == 1:
            y_arrived(z)
            for q in range(1, nout):
                a_arrived(((o + q) % nout) * ncol + x)
                for d in range(1, ncol):
                    a_second(q, d).start()
        elif s < nz - 1:
            for zz in (z - (s - 1), z + (s - 1)):
                @pl.when((zz >= 0) & (zz < nz) & (zz != mate))
                def _():
                    y_arrived(zz)
        if s == max(nz - 2, 1):
            for h in range(BY_Y, PIECES):
                extra(h, lambda c: c.start())

    local_g.wait()
    local_a.wait()
    for d in range(1, ncol):
        for q in range(nout):
            a_arrived(((o + q) % nout) * ncol + (x + d) % ncol)
    for zz in range(nz):
        for h in range(PIECES):
            arrived(op, zz, h)
    tile = min(512, piece)
    per_piece = piece // tile

    def dots(yy, columns):
        total = None
        for k in range(2 * ncol):
            block = yy * 2 * ncol + k
            part = jnp.dot(
                av[block],
                gs[pl.ds(pl.multiple_of(block * ta, ta), ta), columns],
                preferred_element_type=jnp.float32,
            )
            total = part if total is None else total + part
        return total

    @pl.loop(0, width // tile)
    def _(j):
        columns = pl.ds(pl.multiple_of(j * tile, tile), tile)
        acc[:, columns] = dots(y, columns)

    rowp[...] = jnp.zeros_like(rowp)
    od = (1 - y) * 2 + (1 - core)
    def finish_piece(h):
        for zz in range(nz):
            arrived(od, zz, h)

        @pl.loop(h * per_piece, (h + 1) * per_piece)
        def _(j):
            columns = pl.ds(pl.multiple_of(j * tile, tile), tile)
            grad = (acc[:, columns] + dots(1 - y, columns)) * scale
            acc[:, columns] = grad
            squares = grad * grad
            part = squares[:, :128]
            for i in range(1, tile // 128):
                part = part + squares[:, i * 128 : (i + 1) * 128]
            rowp[...] += part
            colbuf[0, :, columns] = jnp.sum(squares, axis=0, keepdims=True)

    for h in range(PIECES):
        for s in range(nz - 2, nz):
            if s > 1 or (s == 1 and nz == 2):
                for zz in (z - s, z + s):
                    @pl.when((zz >= 0) & (zz < nz) & (zz != mate))
                    def _():
                        here = arrived(oy, zz, h)
                        to_partner(here, oy, zz, h).start()

        here = arrived(oy, mate, h)
        to_partner(here, oy, mate, h).start()
        if h > 0:
            finish_piece(h - 1)
    finish_piece(PIECES - 1)

    out_copy = pltpu.make_async_copy(acc, grad_hbm, out_sem)
    out_copy.start()

    def c_first(d):
        return remote(colbuf.at[0], colbuf.at[nout - d], c_send.at[d], c_recv.at[nout - d], {"outer": (o + d) % nout})

    def c_second(d):
        return remote(colz.at[0], colz.at[nz - d], cz_send.at[d], cz_recv.at[nz - d], {"row": (z + d) % nz})

    def r_first(d):
        return remote(rowbuf.at[0], rowbuf.at[ncol - d], r_send.at[d], r_recv.at[ncol - d], {"col": (x + d) % ncol})

    def t_first(d):
        return remote(totz.at[0], totz.at[nz - d], tz_send.at[d], tz_recv.at[nz - d], {"row": (z + d) % nz})

    def t_second(d):
        return remote(toto.at[0], toto.at[nout - d], to_send.at[d], to_recv.at[nout - d], {"outer": (o + d) % nout})

    def finish(copies):
        for c in copies:
            c.wait()

    firsts = [c_first(d) for d in range(1, nout)]
    for c in firsts:
        c.start()
    rowbuf[0] = jnp.sum(jnp.transpose(rowp[...]), axis=0, keepdims=True)
    rights = [r_first(d) for d in range(1, ncol)]
    for c in rights:
        c.start()
    finish(rights)
    row_sq = rowbuf[0]
    for d in range(1, ncol):
        row_sq = row_sq + rowbuf[d]
    new_row = decay * rm_ref[...] + (1.0 - decay) * row_sq / F
    nr_ref[...] = new_row
    totz[0] = jnp.broadcast_to(jnp.sum(new_row, axis=1, keepdims=True), totz.shape[1:])
    tots = [t_first(d) for d in range(1, nz)]
    for c in tots:
        c.start()
    finish(firsts)
    col_sq = colbuf[0]
    for d in range(1, nout):
        col_sq = col_sq + colbuf[d]
    colz[0] = col_sq
    seconds = [c_second(d) for d in range(1, nz)]
    for c in seconds:
        c.start()
    finish(tots)
    total = totz[0]
    for d in range(1, nz):
        total = total + totz[d]
    toto[0] = total
    lasts = [t_second(d) for d in range(1, nout)]
    for c in lasts:
        c.start()
    finish(seconds)
    col_sq = colz[0]
    for d in range(1, nz):
        col_sq = col_sq + colz[d]
    nc_ref[...] = decay * cm_ref[...] + (1.0 - decay) * col_sq / D
    finish(lasts)
    total = toto[0]
    for d in range(1, nout):
        total = total + toto[d]
    mt_ref[...] = total

    for h in range(PIECES):
        for zz in range(nz):
            @pl.when((z < nz - 1) & (zz <= z))
            def _():
                to_up(place(slot(o, zz), h), o, zz, h).wait_send()

            @pl.when((z > 0) & (zz >= z))
            def _():
                to_down(place(slot(o, zz), h), o, zz, h).wait_send()

            @pl.when((zz != mate) | (h < BY_Y))
            def _():
                to_y(place(slot(o, zz), h), zz, h).wait_send()

            to_partner(place(slot(o, zz), h), o, zz, h).wait_send()
            to_partner(place(slot(oy, zz), h), oy, zz, h).wait_send()
        if h >= BY_Y:
            extra(h, lambda c: c.wait_send())
    for d in range(1, nout):
        a_first(d).wait_send()
    for q in range(nout):
        for d in range(1, ncol):
            a_second(q, d).wait_send()
    out_copy.wait()


def body(nout, nz, ncol, activations, out_grads, row_moment, col_moment):
    rows, width = row_moment.shape[0], col_moment.shape[0]
    ta, tg = activations.shape[0], out_grads.shape[0]
    tokens = ta * ncol * nout
    decay = 1.0 - STEP ** (-0.8)
    turned = activations.T.reshape(nout, rows, ta)
    f32, bf16 = jnp.float32, jnp.bfloat16
    vmem = pl.BlockSpec(memory_space=pltpu.VMEM)
    dma = pltpu.SemaphoreType.DMA
    grad, new_row, new_col, total = pl.pallas_call(
        functools.partial(kernel, nout, nz, ncol, 1.0 / tokens**0.5, decay),
        out_shape=(
            jax.ShapeDtypeStruct((rows, width), f32),
            jax.ShapeDtypeStruct((1, rows), f32),
            jax.ShapeDtypeStruct((1, width), f32),
            jax.ShapeDtypeStruct((1, 128), f32),
        ),
        in_specs=[vmem] * 4,
        out_specs=(pl.BlockSpec(memory_space=pl.ANY), vmem, vmem, vmem),
        scratch_shapes=[
            pltpu.VMEM((tokens, width), bf16),
            pltpu.VMEM((nout * ncol, rows, ta), bf16),
            pltpu.VMEM((rows, width), f32),
            pltpu.VMEM((rows, 128), f32),
            pltpu.VMEM((nout, 1, width), f32),
            pltpu.VMEM((nz, 1, width), f32),
            pltpu.VMEM((ncol, 1, rows), f32),
            pltpu.VMEM((nz, 1, 128), f32),
            pltpu.VMEM((nout, 1, 128), f32),
            dma((nout * nz, PIECES)),
            dma((nz + 1, PIECES)),
            dma((nz + 1, PIECES)),
            dma((nz, PIECES)),
            dma((2 * nz, PIECES)),
            dma((nout * ncol,)),
            dma((nout,)),
            dma((nout, ncol)),
            dma((2,)),
            dma,
            dma((nout,)), dma((nout,)),
            dma((nz,)), dma((nz,)),
            dma((ncol,)), dma((ncol,)),
            dma((nz,)), dma((nz,)),
            dma((nout,)), dma((nout,)),
        ],
        compiler_params=pltpu.CompilerParams(
            collective_id=0, has_side_effects=True, vmem_limit_bytes=44 * 1024 * 1024
        ),
    )(turned, out_grads, row_moment.reshape(1, rows), col_moment.reshape(1, width))
    factor = lax.rsqrt(new_row.reshape(rows)[:, None] * new_col * (D / total[0, 0]))
    update = (grad * factor).astype(bf16)
    return (update, new_row.reshape(rows), new_col.reshape(width))


def solution(mesh):
    nout, nz, ncol = mesh.shape["outer"], mesh.shape["row"], mesh.shape["col"]
    return jax.shard_map(
        functools.partial(body, nout, nz, ncol),
        mesh=mesh,
        in_specs=(
            P(("outer", "col"), "row"),
            P(("outer", "row"), "col"),
            P(("row", "outer")),
            P("col"),
        ),
        out_specs=(P(("row", "outer"), "col"), P(("row", "outer")), P("col")),
        check_vma=False,
    )
```

```python
import functools

import jax
import jax.numpy as jnp
from jax import lax
from jax.experimental import pallas as pl
from jax.experimental.pallas import tpu as pltpu
from jax.sharding import PartitionSpec as P

D = 9216
F = 8192
STEP = 2
MESH = pl.DeviceIdType.MESH
PIECES = 4
BY_Y = 1


def kernel(
    nout, nz, ncol, scale, decay,
    a_ref, g_ref, rm_ref, cm_ref,
    acc, nr_ref, nrc_ref, nc_ref, mt_ref,
    gs, av, rowp, colbuf, colz, rowbuf, totz, toto,
    g_recv, zp_send, zm_send, y_send, p_send, a_recv, a1_send, a2_send, loc_sem,
    c_send, c_recv, cz_send, cz_recv, r_send, r_recv, tz_send, tz_recv, to_send, to_recv,
):
    tg, width = g_ref.shape
    rows, ta = av.shape[1], av.shape[2]
    piece = width // PIECES
    o = lax.axis_index("outer")
    z = lax.axis_index("row")
    x = lax.axis_index("col")
    y, core = o // 2, o % 2
    oy = (1 - y) * 2 + core
    op = y * 2 + (1 - core)
    mate = z + 1 - 2 * (z % 2)

    def remote(src, dst, s, r, dev):
        return pltpu.make_async_remote_copy(
            src_ref=src, dst_ref=dst, send_sem=s, recv_sem=r, device_id=dev, device_id_type=MESH
        )

    barrier = pltpu.get_barrier_semaphore()
    for d in range(1, nout):
        pl.semaphore_signal(barrier, inc=1, device_id={"outer": (o + d) % nout}, device_id_type=MESH)

    @pl.when(z > 0)
    def _():
        pl.semaphore_signal(barrier, inc=1, device_id={"row": jnp.maximum(z - 1, 0)}, device_id_type=MESH)

    @pl.when(z < nz - 1)
    def _():
        pl.semaphore_signal(barrier, inc=1, device_id={"row": jnp.minimum(z + 1, nz - 1)}, device_id_type=MESH)

    for d in range(1, ncol):
        pl.semaphore_signal(barrier, inc=1, device_id={"col": (x + d) % ncol}, device_id_type=MESH)
    ends = jnp.where(z > 0, 1, 0) + jnp.where(z < nz - 1, 1, 0)
    pl.semaphore_wait(barrier, nout + ncol - 2 + ends)

    def slot(oo, zz):
        return oo * nz + zz

    def place(s, h):
        return gs.at[pl.ds(pl.multiple_of(s * tg, tg), tg), pl.ds(h * piece, piece)]

    def g_copy(src, s, h, sem, dev):
        return remote(src, place(s, h), sem, g_recv.at[s, h], dev)

    def to_up(src, oo, zz, h):
        k = jnp.where(oo == o, zz, nz)
        return g_copy(src, slot(oo, zz), h, zp_send.at[k, h], {"row": jnp.minimum(z + 1, nz - 1)})

    def to_down(src, oo, zz, h):
        k = jnp.where(oo == o, zz, nz)
        return g_copy(src, slot(oo, zz), h, zm_send.at[k, h], {"row": jnp.maximum(z - 1, 0)})

    def to_y(src, zz, h):
        return g_copy(src, slot(o, zz), h, y_send.at[zz, h], {"outer": oy})

    def to_partner(src, oo, zz, h):
        k = jnp.where(oo == o, zz, nz + zz)
        return g_copy(src, slot(oo, zz), h, p_send.at[k, h], {"outer": op})

    def arrived(oo, zz, h):
        here = place(slot(oo, zz), h)
        to_partner(here, oo, zz, h).wait_recv()
        return here

    own = [g_ref.at[:, pl.ds(h * piece, piece)] for h in range(PIECES)]
    for h in range(PIECES):
        @pl.when(z < nz - 1)
        def _():
            to_up(own[h], o, z, h).start()

        @pl.when(z > 0)
        def _():
            to_down(own[h], o, z, h).start()

        to_y(own[h], z, h).start()
        to_partner(own[h], o, z, h).start()

    def a_first(d):
        target = (o + d) % nout
        return remote(a_ref.at[target], av.at[o * ncol + x], a1_send.at[d], a_recv.at[o * ncol + x], {"outer": target})

    def a_second(q, d):
        oo = (o + q) % nout
        k = oo * ncol + x
        src = a_ref.at[o] if q == 0 else av.at[k]
        return remote(src, av.at[k], a2_send.at[q, d], a_recv.at[k], {"col": (x + d) % ncol})

    for d in range(1, nout):
        a_first(d).start()
    for d in range(1, ncol):
        a_second(0, d).start()
    local_g = pltpu.make_async_copy(g_ref, gs.at[pl.ds(pl.multiple_of(slot(o, z) * tg, tg), tg), :], loc_sem.at[0])
    local_a = pltpu.make_async_copy(a_ref.at[o], av.at[o * ncol + x], loc_sem.at[1])
    local_g.start()
    local_a.start()

    def a_arrived(k):
        remote(av.at[k], av.at[k], a1_send.at[1], a_recv.at[k], {"outer": oy}).wait_recv()

    def y_arrived(zz, forward=False):
        for h in range(PIECES):
            here = arrived(oy, zz, h)
            to_partner(here, oy, zz, h).start()

    def extra(h, act):
        here = place(slot(oy, z), h)

        @pl.when(mate > z)
        def _():
            act(to_up(here, oy, z, h))

        @pl.when(mate < z)
        def _():
            act(to_down(here, oy, z, h))

    for s in range(1, nz):
        for h in range(PIECES):
            @pl.when(z - s >= 0)
            def _():
                here = arrived(o, z - s, h)

                @pl.when(z < nz - 1)
                def _():
                    to_up(here, o, z - s, h).start()

                @pl.when((z - s != mate) | (h < BY_Y))
                def _():
                    to_y(here, z - s, h).start()

                to_partner(here, o, z - s, h).start()

            @pl.when(z + s < nz)
            def _():
                here = arrived(o, z + s, h)

                @pl.when(z > 0)
                def _():
                    to_down(here, o, z + s, h).start()

                @pl.when((z + s != mate) | (h < BY_Y))
                def _():
                    to_y(here, z + s, h).start()

                to_partner(here, o, z + s, h).start()

        if s == 1:
            y_arrived(z)
            for q in range(1, nout):
                a_arrived(((o + q) % nout) * ncol + x)
                for d in range(1, ncol):
                    a_second(q, d).start()
        elif s < nz - 1:
            for zz in (z - (s - 1), z + (s - 1)):
                @pl.when((zz >= 0) & (zz < nz) & (zz != mate))
                def _():
                    y_arrived(zz)
        if s == max(nz - 2, 1):
            for h in range(BY_Y, PIECES):
                extra(h, lambda c: c.start())

    local_g.wait()
    local_a.wait()
    for d in range(1, ncol):
        for q in range(nout):
            a_arrived(((o + q) % nout) * ncol + (x + d) % ncol)
    for zz in range(nz):
        for h in range(PIECES):
            arrived(op, zz, h)
    tile = min(512, piece)
    per_piece = piece // tile

    def dots(yy, columns):
        total = None
        for k in range(2 * ncol):
            block = yy * 2 * ncol + k
            part = jnp.dot(
                av[block],
                gs[pl.ds(pl.multiple_of(block * ta, ta), ta), columns],
                preferred_element_type=jnp.float32,
            )
            total = part if total is None else total + part
        return total

    @pl.loop(0, width // tile)
    def _(j):
        columns = pl.ds(pl.multiple_of(j * tile, tile), tile)
        acc[:, columns] = dots(y, columns)

    rowp[...] = jnp.zeros_like(rowp)
    od = (1 - y) * 2 + (1 - core)
    def finish_piece(h):
        for zz in range(nz):
            arrived(od, zz, h)

        @pl.loop(h * per_piece, (h + 1) * per_piece)
        def _(j):
            columns = pl.ds(pl.multiple_of(j * tile, tile), tile)
            grad = (acc[:, columns] + dots(1 - y, columns)) * scale
            acc[:, columns] = grad
            squares = grad * grad
            part = squares[:, :128]
            for i in range(1, tile // 128):
                part = part + squares[:, i * 128 : (i + 1) * 128]
            rowp[...] += part
            colbuf[0, :, columns] = jnp.sum(squares, axis=0, keepdims=True)

    for h in range(PIECES):
        for s in range(nz - 2, nz):
            if s > 1 or (s == 1 and nz == 2):
                for zz in (z - s, z + s):
                    @pl.when((zz >= 0) & (zz < nz) & (zz != mate))
                    def _():
                        here = arrived(oy, zz, h)
                        to_partner(here, oy, zz, h).start()

        here = arrived(oy, mate, h)
        to_partner(here, oy, mate, h).start()
        if h > 0:
            finish_piece(h - 1)
    finish_piece(PIECES - 1)

    def c_first(d):
        return remote(colbuf.at[0], colbuf.at[nout - d], c_send.at[d], c_recv.at[nout - d], {"outer": (o + d) % nout})

    def c_second(d):
        return remote(colz.at[0], colz.at[nz - d], cz_send.at[d], cz_recv.at[nz - d], {"row": (z + d) % nz})

    def r_first(d):
        return remote(rowbuf.at[0], rowbuf.at[ncol - d], r_send.at[d], r_recv.at[ncol - d], {"col": (x + d) % ncol})

    def t_first(d):
        return remote(toto.at[0], toto.at[nout - d], to_send.at[d], to_recv.at[nout - d], {"outer": (o + d) % nout})

    def t_second(d, e):
        k = ((nz - d) % nz) * ncol + (ncol - e) % ncol
        dev = {"row": (z + d) % nz, "col": (x + e) % ncol}
        return remote(totz.at[0], totz.at[k], tz_send.at[d * ncol + e], tz_recv.at[k], dev)

    def finish(copies):
        for c in copies:
            c.wait()

    firsts = [c_first(d) for d in range(1, nout)]
    for c in firsts:
        c.start()
    mine = jnp.sum(jnp.transpose(rowp[...]), axis=0, keepdims=True)
    rowbuf[0] = mine
    rights = [r_first(d) for d in range(1, ncol)]
    for c in rights:
        c.start()
    share = (decay / ncol) * rm_ref[...] + ((1.0 - decay) / F) * mine
    toto[0] = jnp.broadcast_to(jnp.sum(share, axis=1, keepdims=True), toto.shape[1:])
    tots = [t_first(d) for d in range(1, nout)]
    for c in tots:
        c.start()
    finish(firsts)
    col_sq = colbuf[0]
    for d in range(1, nout):
        col_sq = col_sq + colbuf[d]
    colz[0] = col_sq
    finish(rights)
    seconds = [c_second(d) for d in range(1, nz)]
    for c in seconds:
        c.start()
    finish(tots)
    total = toto[0]
    for d in range(1, nout):
        total = total + toto[d]
    totz[0] = total
    lasts = [t_second(d, e) for d in range(nz) for e in range(ncol) if d + e > 0]
    for c in lasts:
        c.start()
    row_sq = rowbuf[0]
    for d in range(1, ncol):
        row_sq = row_sq + rowbuf[d]
    new_row = decay * rm_ref[...] + (1.0 - decay) * row_sq / F
    nr_ref[...] = new_row
    nrc_ref[...] = jnp.transpose(jnp.broadcast_to(new_row, (128, new_row.shape[1])))
    finish(seconds)
    col_sq = colz[0]
    for d in range(1, nz):
        col_sq = col_sq + colz[d]
    nc_ref[...] = decay * cm_ref[...] + (1.0 - decay) * col_sq / D
    finish(lasts)
    total = totz[0]
    for k in range(1, nz * ncol):
        total = total + totz[k]
    mt_ref[...] = total

    for h in range(PIECES):
        for zz in range(nz):
            @pl.when((z < nz - 1) & (zz <= z))
            def _():
                to_up(place(slot(o, zz), h), o, zz, h).wait_send()

            @pl.when((z > 0) & (zz >= z))
            def _():
                to_down(place(slot(o, zz), h), o, zz, h).wait_send()

            @pl.when((zz != mate) | (h < BY_Y))
            def _():
                to_y(place(slot(o, zz), h), zz, h).wait_send()

            to_partner(place(slot(o, zz), h), o, zz, h).wait_send()
            to_partner(place(slot(oy, zz), h), oy, zz, h).wait_send()
        if h >= BY_Y:
            extra(h, lambda c: c.wait_send())
    for d in range(1, nout):
        a_first(d).wait_send()
    for q in range(nout):
        for d in range(1, ncol):
            a_second(q, d).wait_send()


def update_kernel(step, grad_ref, nr_ref, nc_ref, mt_ref, out_ref):
    here = pl.ds(pl.multiple_of(pl.program_id(0) * step, step), step)
    scale = D / mt_ref[0, 0]
    factor = lax.rsqrt(nr_ref[here, :1] * nc_ref[...] * scale)
    out_ref[...] = (grad_ref[here, :] * factor).astype(out_ref.dtype)


def body(nout, nz, ncol, activations, out_grads, row_moment, col_moment):
    rows, width = row_moment.shape[0], col_moment.shape[0]
    ta, tg = activations.shape[0], out_grads.shape[0]
    tokens = ta * ncol * nout
    decay = 1.0 - STEP ** (-0.8)
    turned = activations.T.reshape(nout, rows, ta)
    f32, bf16 = jnp.float32, jnp.bfloat16
    vmem = pl.BlockSpec(memory_space=pltpu.VMEM)
    dma = pltpu.SemaphoreType.DMA
    grad, new_row, turned_row, new_col, total = pl.pallas_call(
        functools.partial(kernel, nout, nz, ncol, 1.0 / tokens**0.5, decay),
        out_shape=(
            pltpu.VMEM((rows, width), f32),
            jax.ShapeDtypeStruct((1, rows), f32),
            pltpu.VMEM((rows, 128), f32),
            jax.ShapeDtypeStruct((1, width), f32),
            jax.ShapeDtypeStruct((1, 128), f32),
        ),
        in_specs=[vmem, pl.BlockSpec(memory_space=pl.ANY), vmem, vmem],
        out_specs=(vmem,) * 5,
        scratch_shapes=[
            pltpu.VMEM((tokens, width), bf16),
            pltpu.VMEM((nout * ncol, rows, ta), bf16),
            pltpu.VMEM((rows, 128), f32),
            pltpu.VMEM((nout, 1, width), f32),
            pltpu.VMEM((nz, 1, width), f32),
            pltpu.VMEM((ncol, 1, rows), f32),
            pltpu.VMEM((nz * ncol, 1, 128), f32),
            pltpu.VMEM((nout, 1, 128), f32),
            dma((nout * nz, PIECES)),
            dma((nz + 1, PIECES)),
            dma((nz + 1, PIECES)),
            dma((nz, PIECES)),
            dma((2 * nz, PIECES)),
            dma((nout * ncol,)),
            dma((nout,)),
            dma((nout, ncol)),
            dma((2,)),
            dma((nout,)), dma((nout,)),
            dma((nz,)), dma((nz,)),
            dma((ncol,)), dma((ncol,)),
            dma((nz * ncol,)), dma((nz * ncol,)),
            dma((nout,)), dma((nout,)),
        ],
        compiler_params=pltpu.CompilerParams(
            collective_id=0, has_side_effects=True, vmem_limit_bytes=44 * 1024 * 1024
        ),
    )(turned, out_grads, row_moment.reshape(1, rows), col_moment.reshape(1, width))
    parts = next(n for n in (4, 3, 2, 1) if n == 1 or rows % (n * 16) == 0)
    step = rows // parts
    update = pl.pallas_call(
        functools.partial(update_kernel, step),
        grid=(parts,),
        out_shape=jax.ShapeDtypeStruct((rows, width), bf16),
        in_specs=[vmem] * 4,
        out_specs=pl.BlockSpec((step, width), lambda i: (i, 0)),
        compiler_params=pltpu.CompilerParams(vmem_limit_bytes=24 * 1024 * 1024),
    )(grad, turned_row, new_col, total)
    return (update, new_row.reshape(rows), new_col.reshape(width))


def solution(mesh):
    nout, nz, ncol = mesh.shape["outer"], mesh.shape["row"], mesh.shape["col"]
    return jax.shard_map(
        functools.partial(body, nout, nz, ncol),
        mesh=mesh,
        in_specs=(
            P(("outer", "col"), "row"),
            P(("outer", "row"), "col"),
            P(("row", "outer")),
            P("col"),
        ),
        out_specs=(P(("row", "outer"), "col"), P(("row", "outer")), P("col")),
        check_vma=False,
    )
```

```python
import functools

import jax
import jax.numpy as jnp
from jax import lax
from jax.experimental import pallas as pl
from jax.experimental.pallas import tpu as pltpu
from jax.sharding import PartitionSpec as P

D = 9216
F = 8192
STEP = 2
MESH = pl.DeviceIdType.MESH
PIECES = 4
BY_Y = 1


def kernel(
    nout, nz, ncol, scale, decay,
    raw_ref, g_ref, rm_ref, cm_ref,
    acc, nr_ref, nrc_ref, nc_ref, mt_ref,
    gs, av, raw, a_ref, rowp, colbuf, colz, rowbuf, totz, toto,
    g_recv, zp_send, zm_send, y_send, p_send, a_recv, a1_send, a2_send, loc_sem,
    c_send, c_recv, cz_send, cz_recv, r_send, r_recv, tz_send, tz_recv, to_send, to_recv,
):
    tg, width = g_ref.shape
    rows, ta = av.shape[1], av.shape[2]
    piece = width // PIECES
    o = lax.axis_index("outer")
    z = lax.axis_index("row")
    x = lax.axis_index("col")
    y, core = o // 2, o % 2
    oy = (1 - y) * 2 + core
    op = y * 2 + (1 - core)
    mate = z + 1 - 2 * (z % 2)

    def remote(src, dst, s, r, dev):
        return pltpu.make_async_remote_copy(
            src_ref=src, dst_ref=dst, send_sem=s, recv_sem=r, device_id=dev, device_id_type=MESH
        )

    load_a = pltpu.make_async_copy(raw_ref, raw, loc_sem.at[2])
    load_a.start()
    barrier = pltpu.get_barrier_semaphore()
    for d in range(1, nout):
        pl.semaphore_signal(barrier, inc=1, device_id={"outer": (o + d) % nout}, device_id_type=MESH)

    @pl.when(z > 0)
    def _():
        pl.semaphore_signal(barrier, inc=1, device_id={"row": jnp.maximum(z - 1, 0)}, device_id_type=MESH)

    @pl.when(z < nz - 1)
    def _():
        pl.semaphore_signal(barrier, inc=1, device_id={"row": jnp.minimum(z + 1, nz - 1)}, device_id_type=MESH)

    for d in range(1, ncol):
        pl.semaphore_signal(barrier, inc=1, device_id={"col": (x + d) % ncol}, device_id_type=MESH)
    ends = jnp.where(z > 0, 1, 0) + jnp.where(z < nz - 1, 1, 0)
    pl.semaphore_wait(barrier, nout + ncol - 2 + ends)

    def slot(oo, zz):
        return oo * nz + zz

    def place(s, h):
        return gs.at[pl.ds(pl.multiple_of(s * tg, tg), tg), pl.ds(h * piece, piece)]

    def g_copy(src, s, h, sem, dev):
        return remote(src, place(s, h), sem, g_recv.at[s, h], dev)

    def to_up(src, oo, zz, h):
        k = jnp.where(oo == o, zz, nz)
        return g_copy(src, slot(oo, zz), h, zp_send.at[k, h], {"row": jnp.minimum(z + 1, nz - 1)})

    def to_down(src, oo, zz, h):
        k = jnp.where(oo == o, zz, nz)
        return g_copy(src, slot(oo, zz), h, zm_send.at[k, h], {"row": jnp.maximum(z - 1, 0)})

    def to_y(src, zz, h):
        return g_copy(src, slot(o, zz), h, y_send.at[zz, h], {"outer": oy})

    def to_partner(src, oo, zz, h):
        k = jnp.where(oo == o, zz, nz + zz)
        return g_copy(src, slot(oo, zz), h, p_send.at[k, h], {"outer": op})

    def arrived(oo, zz, h):
        here = place(slot(oo, zz), h)
        to_partner(here, oo, zz, h).wait_recv()
        return here

    own = [g_ref.at[:, pl.ds(h * piece, piece)] for h in range(PIECES)]
    for h in range(PIECES):
        @pl.when(z < nz - 1)
        def _():
            to_up(own[h], o, z, h).start()

        @pl.when(z > 0)
        def _():
            to_down(own[h], o, z, h).start()

        to_y(own[h], z, h).start()
        to_partner(own[h], o, z, h).start()

    def a_first(d):
        target = (o + d) % nout
        return remote(a_ref.at[target], av.at[o * ncol + x], a1_send.at[d], a_recv.at[o * ncol + x], {"outer": target})

    def a_second(q, d):
        oo = (o + q) % nout
        k = oo * ncol + x
        src = a_ref.at[o] if q == 0 else av.at[k]
        return remote(src, av.at[k], a2_send.at[q, d], a_recv.at[k], {"col": (x + d) % ncol})

    local_g = pltpu.make_async_copy(g_ref, gs.at[pl.ds(pl.multiple_of(slot(o, z) * tg, tg), tg), :], loc_sem.at[0])
    local_a = pltpu.make_async_copy(a_ref.at[o], av.at[o * ncol + x], loc_sem.at[1])
    local_g.start()
    load_a.wait()
    turned = jnp.transpose(raw[...])
    for k in range(nout):
        a_ref[k] = turned[k * rows : (k + 1) * rows]

    def a_arrived(k):
        remote(av.at[k], av.at[k], a1_send.at[1], a_recv.at[k], {"outer": oy}).wait_recv()

    def y_arrived(zz, forward=False):
        for h in range(PIECES):
            here = arrived(oy, zz, h)
            to_partner(here, oy, zz, h).start()

    def extra(h, act):
        here = place(slot(oy, z), h)

        @pl.when(mate > z)
        def _():
            act(to_up(here, oy, z, h))

        @pl.when(mate < z)
        def _():
            act(to_down(here, oy, z, h))

    for s in range(1, nz):
        for h in range(PIECES):
            @pl.when(z - s >= 0)
            def _():
                here = arrived(o, z - s, h)

                @pl.when(z < nz - 1)
                def _():
                    to_up(here, o, z - s, h).start()

                @pl.when((z - s != mate) | (h < BY_Y))
                def _():
                    to_y(here, z - s, h).start()

                to_partner(here, o, z - s, h).start()

            @pl.when(z + s < nz)
            def _():
                here = arrived(o, z + s, h)

                @pl.when(z > 0)
                def _():
                    to_down(here, o, z + s, h).start()

                @pl.when((z + s != mate) | (h < BY_Y))
                def _():
                    to_y(here, z + s, h).start()

                to_partner(here, o, z + s, h).start()

            if s == 1 and h == 1:
                for d in range(1, nout):
                    a_first(d).start()
                for d in range(1, ncol):
                    a_second(0, d).start()
                local_a.start()

        if s == 1:
            y_arrived(z)
            for q in range(1, nout):
                a_arrived(((o + q) % nout) * ncol + x)
                for d in range(1, ncol):
                    a_second(q, d).start()
        elif s < nz - 1:
            for zz in (z - (s - 1), z + (s - 1)):
                @pl.when((zz >= 0) & (zz < nz) & (zz != mate))
                def _():
                    y_arrived(zz)
        if s == max(nz - 2, 1):
            for h in range(BY_Y, PIECES):
                extra(h, lambda c: c.start())

    local_g.wait()
    local_a.wait()
    for d in range(1, ncol):
        for q in range(nout):
            a_arrived(((o + q) % nout) * ncol + (x + d) % ncol)
    for zz in range(nz):
        for h in range(PIECES):
            arrived(op, zz, h)
    tile = min(512, piece)
    per_piece = piece // tile

    def dots(yy, columns):
        total = None
        for k in range(2 * ncol):
            block = yy * 2 * ncol + k
            part = jnp.dot(
                av[block],
                gs[pl.ds(pl.multiple_of(block * ta, ta), ta), columns],
                preferred_element_type=jnp.float32,
            )
            total = part if total is None else total + part
        return total

    @pl.loop(0, width // tile)
    def _(j):
        columns = pl.ds(pl.multiple_of(j * tile, tile), tile)
        acc[:, columns] = dots(y, columns)

    rowp[...] = jnp.zeros_like(rowp)
    od = (1 - y) * 2 + (1 - core)
    def finish_piece(h):
        for zz in range(nz):
            arrived(od, zz, h)

        @pl.loop(h * per_piece, (h + 1) * per_piece)
        def _(j):
            columns = pl.ds(pl.multiple_of(j * tile, tile), tile)
            grad = (acc[:, columns] + dots(1 - y, columns)) * scale
            acc[:, columns] = grad
            squares = grad * grad
            part = squares[:, :128]
            for i in range(1, tile // 128):
                part = part + squares[:, i * 128 : (i + 1) * 128]
            rowp[...] += part
            colbuf[0, :, columns] = jnp.sum(squares, axis=0, keepdims=True)

    for h in range(PIECES):
        for s in range(nz - 2, nz):
            if s > 1 or (s == 1 and nz == 2):
                for zz in (z - s, z + s):
                    @pl.when((zz >= 0) & (zz < nz) & (zz != mate))
                    def _():
                        here = arrived(oy, zz, h)
                        to_partner(here, oy, zz, h).start()

        here = arrived(oy, mate, h)
        to_partner(here, oy, mate, h).start()
        if h > 0:
            finish_piece(h - 1)
    finish_piece(PIECES - 1)

    def c_first(d):
        return remote(colbuf.at[0], colbuf.at[nout - d], c_send.at[d], c_recv.at[nout - d], {"outer": (o + d) % nout})

    def c_second(d):
        return remote(colz.at[0], colz.at[nz - d], cz_send.at[d], cz_recv.at[nz - d], {"row": (z + d) % nz})

    def r_first(d):
        return remote(rowbuf.at[0], rowbuf.at[ncol - d], r_send.at[d], r_recv.at[ncol - d], {"col": (x + d) % ncol})

    def t_first(d):
        return remote(toto.at[0], toto.at[nout - d], to_send.at[d], to_recv.at[nout - d], {"outer": (o + d) % nout})

    def t_second(d, e):
        k = ((nz - d) % nz) * ncol + (ncol - e) % ncol
        dev = {"row": (z + d) % nz, "col": (x + e) % ncol}
        return remote(totz.at[0], totz.at[k], tz_send.at[d * ncol + e], tz_recv.at[k], dev)

    def finish(copies):
        for c in copies:
            c.wait()

    firsts = [c_first(d) for d in range(1, nout)]
    for c in firsts:
        c.start()
    mine = jnp.sum(jnp.transpose(rowp[...]), axis=0, keepdims=True)
    rowbuf[0] = mine
    rights = [r_first(d) for d in range(1, ncol)]
    for c in rights:
        c.start()
    share = (decay / ncol) * rm_ref[...].reshape(1, rows) + ((1.0 - decay) / F) * mine
    toto[0] = jnp.broadcast_to(jnp.sum(share, axis=1, keepdims=True), toto.shape[1:])
    tots = [t_first(d) for d in range(1, nout)]
    for c in tots:
        c.start()
    finish(firsts)
    col_sq = colbuf[0]
    for d in range(1, nout):
        col_sq = col_sq + colbuf[d]
    colz[0] = col_sq
    finish(rights)
    seconds = [c_second(d) for d in range(1, nz)]
    for c in seconds:
        c.start()
    finish(tots)
    total = toto[0]
    for d in range(1, nout):
        total = total + toto[d]
    totz[0] = total
    lasts = [t_second(d, e) for d in range(nz) for e in range(ncol) if d + e > 0]
    for c in lasts:
        c.start()
    row_sq = rowbuf[0]
    for d in range(1, ncol):
        row_sq = row_sq + rowbuf[d]
    new_row = decay * rm_ref[...].reshape(1, rows) + (1.0 - decay) * row_sq / F
    nr_ref[...] = new_row
    nrc_ref[...] = jnp.transpose(jnp.broadcast_to(new_row, (128, new_row.shape[1])))
    finish(seconds)
    col_sq = colz[0]
    for d in range(1, nz):
        col_sq = col_sq + colz[d]
    nc_ref[...] = decay * cm_ref[...].reshape(1, width) + (1.0 - decay) * col_sq / D
    finish(lasts)
    total = totz[0]
    for k in range(1, nz * ncol):
        total = total + totz[k]
    mt_ref[...] = total

    for h in range(PIECES):
        for zz in range(nz):
            @pl.when((z < nz - 1) & (zz <= z))
            def _():
                to_up(place(slot(o, zz), h), o, zz, h).wait_send()

            @pl.when((z > 0) & (zz >= z))
            def _():
                to_down(place(slot(o, zz), h), o, zz, h).wait_send()

            @pl.when((zz != mate) | (h < BY_Y))
            def _():
                to_y(place(slot(o, zz), h), zz, h).wait_send()

            to_partner(place(slot(o, zz), h), o, zz, h).wait_send()
            to_partner(place(slot(oy, zz), h), oy, zz, h).wait_send()
        if h >= BY_Y:
            extra(h, lambda c: c.wait_send())
    for d in range(1, nout):
        a_first(d).wait_send()
    for q in range(nout):
        for d in range(1, ncol):
            a_second(q, d).wait_send()


def update_kernel(step, grad_ref, nr_ref, nc_ref, mt_ref, flat_ref, out_ref, row_ref, col_ref):
    here = pl.ds(pl.multiple_of(pl.program_id(0) * step, step), step)
    scale = D / mt_ref[0, 0]
    by_row = lax.rsqrt(nr_ref[here, :1])
    by_col = lax.rsqrt(nc_ref[...] * scale)
    @pl.when(pl.program_id(0) == 0)
    def _():
        row_ref[...] = flat_ref[...].reshape(row_ref.shape)
        col_ref[...] = nc_ref[...].reshape(col_ref.shape)

    out_ref[...] = (grad_ref[here, :] * by_row * by_col).astype(out_ref.dtype)


def body(nout, nz, ncol, activations, out_grads, row_moment, col_moment):
    rows, width = row_moment.shape[0], col_moment.shape[0]
    ta, tg = activations.shape[0], out_grads.shape[0]
    tokens = ta * ncol * nout
    decay = 1.0 - STEP ** (-0.8)
    f32, bf16 = jnp.float32, jnp.bfloat16
    vmem = pl.BlockSpec(memory_space=pltpu.VMEM)
    dma = pltpu.SemaphoreType.DMA
    grad, new_row, turned_row, new_col, total = pl.pallas_call(
        functools.partial(kernel, nout, nz, ncol, 1.0 / tokens**0.5, decay),
        out_shape=(
            pltpu.VMEM((rows, width), f32),
            jax.ShapeDtypeStruct((1, rows), f32),
            pltpu.VMEM((rows, 128), f32),
            jax.ShapeDtypeStruct((1, width), f32),
            jax.ShapeDtypeStruct((1, 128), f32),
        ),
        in_specs=[pl.BlockSpec(memory_space=pl.ANY)] * 2 + [vmem] * 2,
        out_specs=(vmem,) * 5,
        scratch_shapes=[
            pltpu.VMEM((tokens, width), bf16),
            pltpu.VMEM((nout * ncol, rows, ta), bf16),
            pltpu.VMEM(activations.shape, bf16),
            pltpu.VMEM((nout, rows, ta), bf16),
            pltpu.VMEM((rows, 128), f32),
            pltpu.VMEM((nout, 1, width), f32),
            pltpu.VMEM((nz, 1, width), f32),
            pltpu.VMEM((ncol, 1, rows), f32),
            pltpu.VMEM((nz * ncol, 1, 128), f32),
            pltpu.VMEM((nout, 1, 128), f32),
            dma((nout * nz, PIECES)),
            dma((nz + 1, PIECES)),
            dma((nz + 1, PIECES)),
            dma((nz, PIECES)),
            dma((2 * nz, PIECES)),
            dma((nout * ncol,)),
            dma((nout,)),
            dma((nout, ncol)),
            dma((3,)),
            dma((nout,)), dma((nout,)),
            dma((nz,)), dma((nz,)),
            dma((ncol,)), dma((ncol,)),
            dma((nz * ncol,)), dma((nz * ncol,)),
            dma((nout,)), dma((nout,)),
        ],
        compiler_params=pltpu.CompilerParams(
            collective_id=0, has_side_effects=True, vmem_limit_bytes=44 * 1024 * 1024
        ),
    )(activations, out_grads, row_moment, col_moment)
    parts = next(n for n in (4, 3, 2, 1) if n == 1 or rows % (n * 16) == 0)
    step = rows // parts
    update, flat_row, flat_col = pl.pallas_call(
        functools.partial(update_kernel, step),
        grid=(parts,),
        out_shape=(
            jax.ShapeDtypeStruct((rows, width), bf16),
            jax.ShapeDtypeStruct((rows,), f32),
            jax.ShapeDtypeStruct((width,), f32),
        ),
        in_specs=[vmem] * 5,
        out_specs=(pl.BlockSpec((step, width), lambda i: (i, 0)), vmem, vmem),
        compiler_params=pltpu.CompilerParams(vmem_limit_bytes=24 * 1024 * 1024),
    )(grad, turned_row, new_col, total, new_row)
    return (update, flat_row, flat_col)


def solution(mesh):
    nout, nz, ncol = mesh.shape["outer"], mesh.shape["row"], mesh.shape["col"]
    return jax.shard_map(
        functools.partial(body, nout, nz, ncol),
        mesh=mesh,
        in_specs=(
            P(("outer", "col"), "row"),
            P(("outer", "row"), "col"),
            P(("row", "outer")),
            P("col"),
        ),
        out_specs=(P(("row", "outer"), "col"), P(("row", "outer")), P("col")),
        check_vma=False,
    )
```

```python
import functools

import jax
import jax.numpy as jnp
from jax import lax
from jax.experimental import pallas as pl
from jax.experimental.pallas import tpu as pltpu
from jax.sharding import PartitionSpec as P

D = 9216
F = 8192
STEP = 2
MESH = pl.DeviceIdType.MESH
PIECES = 4
BY_Y = 1


def kernel(
    nout, nz, ncol, scale, decay,
    raw_ref, g_ref, rm_hbm, cm_hbm,
    acc, nr_ref, nrc_ref, nc_ref, mt_ref,
    gs, av, raw, a_ref, rm_ref, cm_ref, rowp, colbuf, colz, rowbuf, totz, toto,
    g_recv, zp_send, zm_send, y_send, p_send, a_recv, a1_send, a2_send, loc_sem,
    c_send, c_recv, cz_send, cz_recv, r_send, r_recv, tz_send, tz_recv, to_send, to_recv,
):
    tg, width = g_ref.shape
    rows, ta = av.shape[1], av.shape[2]
    piece = width // PIECES
    o = lax.axis_index("outer")
    z = lax.axis_index("row")
    x = lax.axis_index("col")
    y, core = o // 2, o % 2
    oy = (1 - y) * 2 + core
    op = y * 2 + (1 - core)
    mate = z + 1 - 2 * (z % 2)

    def remote(src, dst, s, r, dev):
        return pltpu.make_async_remote_copy(
            src_ref=src, dst_ref=dst, send_sem=s, recv_sem=r, device_id=dev, device_id_type=MESH
        )

    load_a = pltpu.make_async_copy(raw_ref, raw, loc_sem.at[2])
    load_a.start()
    load_rm = pltpu.make_async_copy(rm_hbm, rm_ref, loc_sem.at[3])
    load_cm = pltpu.make_async_copy(cm_hbm, cm_ref, loc_sem.at[4])
    load_rm.start()
    load_cm.start()
    barrier = pltpu.get_barrier_semaphore()
    for d in range(1, nout):
        pl.semaphore_signal(barrier, inc=1, device_id={"outer": (o + d) % nout}, device_id_type=MESH)

    @pl.when(z > 0)
    def _():
        pl.semaphore_signal(barrier, inc=1, device_id={"row": jnp.maximum(z - 1, 0)}, device_id_type=MESH)

    @pl.when(z < nz - 1)
    def _():
        pl.semaphore_signal(barrier, inc=1, device_id={"row": jnp.minimum(z + 1, nz - 1)}, device_id_type=MESH)

    for d in range(1, ncol):
        pl.semaphore_signal(barrier, inc=1, device_id={"col": (x + d) % ncol}, device_id_type=MESH)
    ends = jnp.where(z > 0, 1, 0) + jnp.where(z < nz - 1, 1, 0)
    pl.semaphore_wait(barrier, nout + ncol - 2 + ends)

    def slot(oo, zz):
        return oo * nz + zz

    def place(s, h):
        return gs.at[pl.ds(pl.multiple_of(s * tg, tg), tg), pl.ds(h * piece, piece)]

    def g_copy(src, s, h, sem, dev):
        return remote(src, place(s, h), sem, g_recv.at[s, h], dev)

    def to_up(src, oo, zz, h):
        k = jnp.where(oo == o, zz, nz)
        return g_copy(src, slot(oo, zz), h, zp_send.at[k, h], {"row": jnp.minimum(z + 1, nz - 1)})

    def to_down(src, oo, zz, h):
        k = jnp.where(oo == o, zz, nz)
        return g_copy(src, slot(oo, zz), h, zm_send.at[k, h], {"row": jnp.maximum(z - 1, 0)})

    def to_y(src, zz, h):
        return g_copy(src, slot(o, zz), h, y_send.at[zz, h], {"outer": oy})

    def to_partner(src, oo, zz, h):
        k = jnp.where(oo == o, zz, nz + zz)
        return g_copy(src, slot(oo, zz), h, p_send.at[k, h], {"outer": op})

    def arrived(oo, zz, h):
        here = place(slot(oo, zz), h)
        to_partner(here, oo, zz, h).wait_recv()
        return here

    own = [g_ref.at[:, pl.ds(h * piece, piece)] for h in range(PIECES)]
    for h in range(PIECES):
        @pl.when(z < nz - 1)
        def _():
            to_up(own[h], o, z, h).start()

        @pl.when(z > 0)
        def _():
            to_down(own[h], o, z, h).start()

        to_y(own[h], z, h).start()
        to_partner(own[h], o, z, h).start()

    def a_first(d):
        target = (o + d) % nout
        return remote(a_ref.at[target], av.at[o * ncol + x], a1_send.at[d], a_recv.at[o * ncol + x], {"outer": target})

    def a_second(oo, d, own=False):
        k = oo * ncol + x
        src = a_ref.at[o] if own else av.at[k]
        return remote(src, av.at[k], a2_send.at[oo, d], a_recv.at[k], {"col": (x + d) % ncol})

    local_g = pltpu.make_async_copy(g_ref, gs.at[pl.ds(pl.multiple_of(slot(o, z) * tg, tg), tg), :], loc_sem.at[0])
    local_a = pltpu.make_async_copy(a_ref.at[o], av.at[o * ncol + x], loc_sem.at[1])
    local_g.start()
    load_a.wait()
    turned = jnp.transpose(raw[...])
    for k in range(nout):
        a_ref[k] = turned[k * rows : (k + 1) * rows]

    def a_arrived(k):
        remote(av.at[k], av.at[k], a1_send.at[1], a_recv.at[k], {"outer": oy}).wait_recv()

    def pass_on(oo):
        a_arrived(oo * ncol + x)
        for d in range(1, ncol):
            a_second(oo, d).start()

    def y_arrived(zz):
        for h in range(PIECES):
            here = arrived(oy, zz, h)
            to_partner(here, oy, zz, h).start()

    def extra(h, act):
        here = place(slot(oy, z), h)

        @pl.when(mate > z)
        def _():
            act(to_up(here, oy, z, h))

        @pl.when(mate < z)
        def _():
            act(to_down(here, oy, z, h))

    for s in range(1, nz):
        for h in range(PIECES):
            @pl.when(z - s >= 0)
            def _():
                here = arrived(o, z - s, h)

                @pl.when(z < nz - 1)
                def _():
                    to_up(here, o, z - s, h).start()

                @pl.when((z - s != mate) | (h < BY_Y))
                def _():
                    to_y(here, z - s, h).start()

                to_partner(here, o, z - s, h).start()

            @pl.when(z + s < nz)
            def _():
                here = arrived(o, z + s, h)

                @pl.when(z > 0)
                def _():
                    to_down(here, o, z + s, h).start()

                @pl.when((z + s != mate) | (h < BY_Y))
                def _():
                    to_y(here, z + s, h).start()

                to_partner(here, o, z + s, h).start()

            if s == 1 and h == 0:
                for d in range(1, nout):
                    a_first(d).start()
                for d in range(1, ncol):
                    a_second(o, d, True).start()
                local_a.start()

        if s == 1:
            y_arrived(z)
            pass_on(op)
        if s == min(2, nz - 1):
            for c in range(2):
                pass_on((1 - y) * 2 + c)
        if 1 < s < nz - 1:
            for zz in (z - (s - 1), z + (s - 1)):
                @pl.when((zz >= 0) & (zz < nz) & (zz != mate))
                def _():
                    y_arrived(zz)
        if s == max(nz - 2, 1):
            for h in range(BY_Y, PIECES):
                extra(h, lambda c: c.start())

    local_g.wait()
    local_a.wait()
    load_rm.wait()
    load_cm.wait()
    for d in range(1, ncol):
        for q in range(nout):
            a_arrived(((o + q) % nout) * ncol + (x + d) % ncol)
    for zz in range(nz):
        for h in range(PIECES):
            arrived(op, zz, h)
    tile = min(512, piece)
    per_piece = piece // tile

    def dots(yy, columns):
        total = None
        for k in range(2 * ncol):
            block = yy * 2 * ncol + k
            part = jnp.dot(
                av[block],
                gs[pl.ds(pl.multiple_of(block * ta, ta), ta), columns],
                preferred_element_type=jnp.float32,
            )
            total = part if total is None else total + part
        return total

    @pl.loop(0, width // tile)
    def _(j):
        columns = pl.ds(pl.multiple_of(j * tile, tile), tile)
        acc[:, columns] = dots(y, columns)

    rowp[...] = jnp.zeros_like(rowp)
    od = (1 - y) * 2 + (1 - core)
    def finish_piece(h):
        for zz in range(nz):
            arrived(od, zz, h)

        @pl.loop(h * per_piece, (h + 1) * per_piece)
        def _(j):
            columns = pl.ds(pl.multiple_of(j * tile, tile), tile)
            grad = (acc[:, columns] + dots(1 - y, columns)) * scale
            acc[:, columns] = grad
            squares = grad * grad
            part = squares[:, :128]
            for i in range(1, tile // 128):
                part = part + squares[:, i * 128 : (i + 1) * 128]
            rowp[...] += part
            colbuf[0, :, columns] = jnp.sum(squares, axis=0, keepdims=True)

    for h in range(PIECES):
        for s in range(nz - 2, nz):
            if s > 1 or (s == 1 and nz == 2):
                for zz in (z - s, z + s):
                    @pl.when((zz >= 0) & (zz < nz) & (zz != mate))
                    def _():
                        here = arrived(oy, zz, h)
                        to_partner(here, oy, zz, h).start()

        here = arrived(oy, mate, h)
        to_partner(here, oy, mate, h).start()
        if h > 0:
            finish_piece(h - 1)
    finish_piece(PIECES - 1)

    def c_first(d):
        return remote(colbuf.at[0], colbuf.at[nout - d], c_send.at[d], c_recv.at[nout - d], {"outer": (o + d) % nout})

    def c_second(d):
        return remote(colz.at[0], colz.at[nz - d], cz_send.at[d], cz_recv.at[nz - d], {"row": (z + d) % nz})

    def r_first(d):
        return remote(rowbuf.at[0], rowbuf.at[ncol - d], r_send.at[d], r_recv.at[ncol - d], {"col": (x + d) % ncol})

    def t_first(d):
        return remote(toto.at[0], toto.at[nout - d], to_send.at[d], to_recv.at[nout - d], {"outer": (o + d) % nout})

    def t_second(d, e):
        k = ((nz - d) % nz) * ncol + (ncol - e) % ncol
        dev = {"row": (z + d) % nz, "col": (x + e) % ncol}
        return remote(totz.at[0], totz.at[k], tz_send.at[d * ncol + e], tz_recv.at[k], dev)

    def finish(copies):
        for c in copies:
            c.wait()

    firsts = [c_first(d) for d in range(1, nout)]
    for c in firsts:
        c.start()
    mine = jnp.sum(jnp.transpose(rowp[...]), axis=0, keepdims=True)
    rowbuf[0] = mine
    rights = [r_first(d) for d in range(1, ncol)]
    for c in rights:
        c.start()
    share = (decay / ncol) * rm_ref[...].reshape(1, rows) + ((1.0 - decay) / F) * mine
    toto[0] = jnp.broadcast_to(jnp.sum(share, axis=1, keepdims=True), toto.shape[1:])
    tots = [t_first(d) for d in range(1, nout)]
    for c in tots:
        c.start()
    finish(firsts)
    col_sq = colbuf[0]
    for d in range(1, nout):
        col_sq = col_sq + colbuf[d]
    colz[0] = col_sq
    finish(rights)
    seconds = [c_second(d) for d in range(1, nz)]
    for c in seconds:
        c.start()
    finish(tots)
    total = toto[0]
    for d in range(1, nout):
        total = total + toto[d]
    totz[0] = total
    lasts = [t_second(d, e) for d in range(nz) for e in range(ncol) if d + e > 0]
    for c in lasts:
        c.start()
    row_sq = rowbuf[0]
    for d in range(1, ncol):
        row_sq = row_sq + rowbuf[d]
    new_row = decay * rm_ref[...].reshape(1, rows) + (1.0 - decay) * row_sq / F
    nr_ref[...] = new_row
    nrc_ref[...] = jnp.transpose(jnp.broadcast_to(new_row, (128, new_row.shape[1])))
    finish(seconds)
    col_sq = colz[0]
    for d in range(1, nz):
        col_sq = col_sq + colz[d]
    nc_ref[...] = decay * cm_ref[...].reshape(1, width) + (1.0 - decay) * col_sq / D
    finish(lasts)
    total = totz[0]
    for k in range(1, nz * ncol):
        total = total + totz[k]
    mt_ref[...] = total

    for h in range(PIECES):
        for zz in range(nz):
            @pl.when((z < nz - 1) & (zz <= z))
            def _():
                to_up(place(slot(o, zz), h), o, zz, h).wait_send()

            @pl.when((z > 0) & (zz >= z))
            def _():
                to_down(place(slot(o, zz), h), o, zz, h).wait_send()

            @pl.when((zz != mate) | (h < BY_Y))
            def _():
                to_y(place(slot(o, zz), h), zz, h).wait_send()

            to_partner(place(slot(o, zz), h), o, zz, h).wait_send()
            to_partner(place(slot(oy, zz), h), oy, zz, h).wait_send()
        if h >= BY_Y:
            extra(h, lambda c: c.wait_send())
    for d in range(1, nout):
        a_first(d).wait_send()
    for oo in range(nout):
        for d in range(1, ncol):
            a_second(oo, d).wait_send()


def update_kernel(step, grad_ref, nr_ref, nc_ref, mt_ref, flat_ref, out_ref, row_ref, col_ref):
    here = pl.ds(pl.multiple_of(pl.program_id(0) * step, step), step)
    scale = D / mt_ref[0, 0]
    by_row = lax.rsqrt(nr_ref[here, :1])
    by_col = lax.rsqrt(nc_ref[...] * scale)
    @pl.when(pl.program_id(0) == 0)
    def _():
        row_ref[...] = flat_ref[...].reshape(row_ref.shape)
        col_ref[...] = nc_ref[...].reshape(col_ref.shape)

    out_ref[...] = (grad_ref[here, :] * by_row * by_col).astype(out_ref.dtype)


def body(nout, nz, ncol, activations, out_grads, row_moment, col_moment):
    rows, width = row_moment.shape[0], col_moment.shape[0]
    ta, tg = activations.shape[0], out_grads.shape[0]
    tokens = ta * ncol * nout
    decay = 1.0 - STEP ** (-0.8)
    f32, bf16 = jnp.float32, jnp.bfloat16
    vmem = pl.BlockSpec(memory_space=pltpu.VMEM)
    dma = pltpu.SemaphoreType.DMA
    grad, new_row, turned_row, new_col, total = pl.pallas_call(
        functools.partial(kernel, nout, nz, ncol, 1.0 / tokens**0.5, decay),
        out_shape=(
            pltpu.VMEM((rows, width), f32),
            jax.ShapeDtypeStruct((1, rows), f32),
            pltpu.VMEM((rows, 128), f32),
            jax.ShapeDtypeStruct((1, width), f32),
            jax.ShapeDtypeStruct((1, 128), f32),
        ),
        in_specs=[pl.BlockSpec(memory_space=pl.ANY)] * 4,
        out_specs=(vmem,) * 5,
        scratch_shapes=[
            pltpu.VMEM((tokens, width), bf16),
            pltpu.VMEM((nout * ncol, rows, ta), bf16),
            pltpu.VMEM(activations.shape, bf16),
            pltpu.VMEM((nout, rows, ta), bf16),
            pltpu.VMEM((rows,), f32),
            pltpu.VMEM((width,), f32),
            pltpu.VMEM((rows, 128), f32),
            pltpu.VMEM((nout, 1, width), f32),
            pltpu.VMEM((nz, 1, width), f32),
            pltpu.VMEM((ncol, 1, rows), f32),
            pltpu.VMEM((nz * ncol, 1, 128), f32),
            pltpu.VMEM((nout, 1, 128), f32),
            dma((nout * nz, PIECES)),
            dma((nz + 1, PIECES)),
            dma((nz + 1, PIECES)),
            dma((nz, PIECES)),
            dma((2 * nz, PIECES)),
            dma((nout * ncol,)),
            dma((nout,)),
            dma((nout, ncol)),
            dma((5,)),
            dma((nout,)), dma((nout,)),
            dma((nz,)), dma((nz,)),
            dma((ncol,)), dma((ncol,)),
            dma((nz * ncol,)), dma((nz * ncol,)),
            dma((nout,)), dma((nout,)),
        ],
        compiler_params=pltpu.CompilerParams(
            collective_id=0, has_side_effects=True, vmem_limit_bytes=44 * 1024 * 1024
        ),
    )(activations, out_grads, row_moment, col_moment)
    parts = next(n for n in (4, 3, 2, 1) if n == 1 or rows % (n * 16) == 0)
    step = rows // parts
    update, flat_row, flat_col = pl.pallas_call(
        functools.partial(update_kernel, step),
        grid=(parts,),
        out_shape=(
            jax.ShapeDtypeStruct((rows, width), bf16),
            jax.ShapeDtypeStruct((rows,), f32),
            jax.ShapeDtypeStruct((width,), f32),
        ),
        in_specs=[vmem] * 5,
        out_specs=(pl.BlockSpec((step, width), lambda i: (i, 0)), vmem, vmem),
        compiler_params=pltpu.CompilerParams(vmem_limit_bytes=24 * 1024 * 1024),
    )(grad, turned_row, new_col, total, new_row)
    return (update, flat_row, flat_col)


def solution(mesh):
    nout, nz, ncol = mesh.shape["outer"], mesh.shape["row"], mesh.shape["col"]
    return jax.shard_map(
        functools.partial(body, nout, nz, ncol),
        mesh=mesh,
        in_specs=(
            P(("outer", "col"), "row"),
            P(("outer", "row"), "col"),
            P(("row", "outer")),
            P("col"),
        ),
        out_specs=(P(("row", "outer"), "col"), P(("row", "outer")), P("col")),
        check_vma=False,
    )
```

```python
import functools

import jax
import jax.numpy as jnp
from jax import lax
from jax.experimental import pallas as pl
from jax.experimental.pallas import tpu as pltpu
from jax.sharding import PartitionSpec as P

D = 9216
F = 8192
STEP = 2
MESH = pl.DeviceIdType.MESH
PIECES = 8
BY_Y = 2


def kernel(
    nout, nz, ncol, scale, decay,
    raw_ref, g_ref, rm_hbm, cm_hbm,
    acc, nr_ref, nrc_ref, nc_ref, mt_ref,
    gs, av, raw, a_ref, rm_ref, cm_ref, rowp, colbuf, colz, rowbuf, totz, toto,
    g_recv, zp_send, zm_send, y_send, p_send, a_recv, a1_send, a2_send, loc_sem,
    c_send, c_recv, cz_send, cz_recv, r_send, r_recv, tz_send, tz_recv, to_send, to_recv,
):
    tg, width = g_ref.shape
    rows, ta = av.shape[1], av.shape[2]
    piece = width // PIECES
    o = lax.axis_index("outer")
    z = lax.axis_index("row")
    x = lax.axis_index("col")
    y, core = o // 2, o % 2
    oy = (1 - y) * 2 + core
    op = y * 2 + (1 - core)
    mate = z + 1 - 2 * (z % 2)

    def remote(src, dst, s, r, dev):
        return pltpu.make_async_remote_copy(
            src_ref=src, dst_ref=dst, send_sem=s, recv_sem=r, device_id=dev, device_id_type=MESH
        )

    load_a = pltpu.make_async_copy(raw_ref, raw, loc_sem.at[2])
    load_a.start()
    load_rm = pltpu.make_async_copy(rm_hbm, rm_ref, loc_sem.at[3])
    load_cm = pltpu.make_async_copy(cm_hbm, cm_ref, loc_sem.at[4])
    load_rm.start()
    load_cm.start()
    barrier = pltpu.get_barrier_semaphore()
    for d in range(1, nout):
        pl.semaphore_signal(barrier, inc=1, device_id={"outer": (o + d) % nout}, device_id_type=MESH)

    @pl.when(z > 0)
    def _():
        pl.semaphore_signal(barrier, inc=1, device_id={"row": jnp.maximum(z - 1, 0)}, device_id_type=MESH)

    @pl.when(z < nz - 1)
    def _():
        pl.semaphore_signal(barrier, inc=1, device_id={"row": jnp.minimum(z + 1, nz - 1)}, device_id_type=MESH)

    for d in range(1, ncol):
        pl.semaphore_signal(barrier, inc=1, device_id={"col": (x + d) % ncol}, device_id_type=MESH)
    ends = jnp.where(z > 0, 1, 0) + jnp.where(z < nz - 1, 1, 0)
    pl.semaphore_wait(barrier, nout + ncol - 2 + ends)

    def slot(oo, zz):
        return oo * nz + zz

    def place(s, h):
        return gs.at[pl.ds(pl.multiple_of(s * tg, tg), tg), pl.ds(h * piece, piece)]

    def g_copy(src, s, h, sem, dev):
        return remote(src, place(s, h), sem, g_recv.at[s, h], dev)

    def to_up(src, oo, zz, h):
        k = jnp.where(oo == o, zz, nz)
        return g_copy(src, slot(oo, zz), h, zp_send.at[k, h], {"row": jnp.minimum(z + 1, nz - 1)})

    def to_down(src, oo, zz, h):
        k = jnp.where(oo == o, zz, nz)
        return g_copy(src, slot(oo, zz), h, zm_send.at[k, h], {"row": jnp.maximum(z - 1, 0)})

    def to_y(src, zz, h):
        return g_copy(src, slot(o, zz), h, y_send.at[zz, h], {"outer": oy})

    def to_partner(src, oo, zz, h):
        k = jnp.where(oo == o, zz, nz + zz)
        return g_copy(src, slot(oo, zz), h, p_send.at[k, h], {"outer": op})

    def arrived(oo, zz, h):
        here = place(slot(oo, zz), h)
        to_partner(here, oo, zz, h).wait_recv()
        return here

    own = [g_ref.at[:, pl.ds(h * piece, piece)] for h in range(PIECES)]
    for h in range(PIECES):
        @pl.when(z < nz - 1)
        def _():
            to_up(own[h], o, z, h).start()

        @pl.when(z > 0)
        def _():
            to_down(own[h], o, z, h).start()

        to_y(own[h], z, h).start()
        to_partner(own[h], o, z, h).start()

    def a_first(d):
        target = (o + d) % nout
        return remote(a_ref.at[target], av.at[o * ncol + x], a1_send.at[d], a_recv.at[o * ncol + x], {"outer": target})

    def a_second(oo, d, own=False):
        k = oo * ncol + x
        src = a_ref.at[o] if own else av.at[k]
        return remote(src, av.at[k], a2_send.at[oo, d], a_recv.at[k], {"col": (x + d) % ncol})

    local_g = pltpu.make_async_copy(g_ref, gs.at[pl.ds(pl.multiple_of(slot(o, z) * tg, tg), tg), :], loc_sem.at[0])
    local_a = pltpu.make_async_copy(a_ref.at[o], av.at[o * ncol + x], loc_sem.at[1])
    local_g.start()
    load_a.wait()
    turned = jnp.transpose(raw[...])
    for k in range(nout):
        a_ref[k] = turned[k * rows : (k + 1) * rows]

    def a_arrived(k):
        remote(av.at[k], av.at[k], a1_send.at[1], a_recv.at[k], {"outer": oy}).wait_recv()

    def pass_on(oo):
        a_arrived(oo * ncol + x)
        for d in range(1, ncol):
            a_second(oo, d).start()

    def y_arrived(zz):
        for h in range(PIECES):
            here = arrived(oy, zz, h)
            to_partner(here, oy, zz, h).start()

    def extra(h, act):
        here = place(slot(oy, z), h)

        @pl.when(mate > z)
        def _():
            act(to_up(here, oy, z, h))

        @pl.when(mate < z)
        def _():
            act(to_down(here, oy, z, h))

    for s in range(1, nz):
        for h in range(PIECES):
            @pl.when(z - s >= 0)
            def _():
                here = arrived(o, z - s, h)

                @pl.when(z < nz - 1)
                def _():
                    to_up(here, o, z - s, h).start()

                @pl.when((z - s != mate) | (h < BY_Y))
                def _():
                    to_y(here, z - s, h).start()

                to_partner(here, o, z - s, h).start()

            @pl.when(z + s < nz)
            def _():
                here = arrived(o, z + s, h)

                @pl.when(z > 0)
                def _():
                    to_down(here, o, z + s, h).start()

                @pl.when((z + s != mate) | (h < BY_Y))
                def _():
                    to_y(here, z + s, h).start()

                to_partner(here, o, z + s, h).start()

            if s == 1 and h == 1:
                for d in range(1, nout):
                    a_first(d).start()
                for d in range(1, ncol):
                    a_second(o, d, True).start()
                local_a.start()

        if s == 1:
            y_arrived(z)
            pass_on(op)
        if s == min(2, nz - 1):
            for c in range(2):
                pass_on((1 - y) * 2 + c)
        if 1 < s < nz - 1:
            for zz in (z - (s - 1), z + (s - 1)):
                @pl.when((zz >= 0) & (zz < nz) & (zz != mate))
                def _():
                    y_arrived(zz)
        if s == max(nz - 2, 1):
            for h in range(BY_Y, PIECES):
                extra(h, lambda c: c.start())

    local_g.wait()
    local_a.wait()
    load_rm.wait()
    load_cm.wait()
    for d in range(1, ncol):
        for q in range(nout):
            a_arrived(((o + q) % nout) * ncol + (x + d) % ncol)
    for zz in range(nz):
        for h in range(PIECES):
            arrived(op, zz, h)
    tile = min(512, piece)
    per_piece = piece // tile

    def dots(yy, columns):
        total = None
        for k in range(2 * ncol):
            block = yy * 2 * ncol + k
            part = jnp.dot(
                av[block],
                gs[pl.ds(pl.multiple_of(block * ta, ta), ta), columns],
                preferred_element_type=jnp.float32,
            )
            total = part if total is None else total + part
        return total

    @pl.loop(0, width // tile)
    def _(j):
        columns = pl.ds(pl.multiple_of(j * tile, tile), tile)
        acc[:, columns] = dots(y, columns)

    rowp[...] = jnp.zeros_like(rowp)
    od = (1 - y) * 2 + (1 - core)
    def finish_piece(h):
        for zz in range(nz):
            arrived(od, zz, h)

        @pl.loop(h * per_piece, (h + 1) * per_piece)
        def _(j):
            columns = pl.ds(pl.multiple_of(j * tile, tile), tile)
            grad = (acc[:, columns] + dots(1 - y, columns)) * scale
            acc[:, columns] = grad
            squares = grad * grad
            part = squares[:, :128]
            for i in range(1, tile // 128):
                part = part + squares[:, i * 128 : (i + 1) * 128]
            rowp[...] += part
            colbuf[0, :, columns] = jnp.sum(squares, axis=0, keepdims=True)

    for h in range(PIECES):
        for s in range(nz - 2, nz):
            if s > 1 or (s == 1 and nz == 2):
                for zz in (z - s, z + s):
                    @pl.when((zz >= 0) & (zz < nz) & (zz != mate))
                    def _():
                        here = arrived(oy, zz, h)
                        to_partner(here, oy, zz, h).start()

        here = arrived(oy, mate, h)
        to_partner(here, oy, mate, h).start()
        if h > 0:
            finish_piece(h - 1)
    finish_piece(PIECES - 1)

    def c_first(d):
        return remote(colbuf.at[0], colbuf.at[nout - d], c_send.at[d], c_recv.at[nout - d], {"outer": (o + d) % nout})

    def c_second(d):
        return remote(colz.at[0], colz.at[nz - d], cz_send.at[d], cz_recv.at[nz - d], {"row": (z + d) % nz})

    def r_first(d):
        return remote(rowbuf.at[0], rowbuf.at[ncol - d], r_send.at[d], r_recv.at[ncol - d], {"col": (x + d) % ncol})

    def t_first(d):
        return remote(toto.at[0], toto.at[nout - d], to_send.at[d], to_recv.at[nout - d], {"outer": (o + d) % nout})

    def t_second(d, e):
        k = ((nz - d) % nz) * ncol + (ncol - e) % ncol
        dev = {"row": (z + d) % nz, "col": (x + e) % ncol}
        return remote(totz.at[0], totz.at[k], tz_send.at[d * ncol + e], tz_recv.at[k], dev)

    def finish(copies):
        for c in copies:
            c.wait()

    firsts = [c_first(d) for d in range(1, nout)]
    for c in firsts:
        c.start()
    mine = jnp.sum(jnp.transpose(rowp[...]), axis=0, keepdims=True)
    rowbuf[0] = mine
    rights = [r_first(d) for d in range(1, ncol)]
    for c in rights:
        c.start()
    share = (decay / ncol) * rm_ref[...].reshape(1, rows) + ((1.0 - decay) / F) * mine
    toto[0] = jnp.broadcast_to(jnp.sum(share, axis=1, keepdims=True), toto.shape[1:])
    tots = [t_first(d) for d in range(1, nout)]
    for c in tots:
        c.start()
    finish(firsts)
    col_sq = colbuf[0]
    for d in range(1, nout):
        col_sq = col_sq + colbuf[d]
    colz[0] = col_sq
    finish(rights)
    seconds = [c_second(d) for d in range(1, nz)]
    for c in seconds:
        c.start()
    finish(tots)
    total = toto[0]
    for d in range(1, nout):
        total = total + toto[d]
    totz[0] = total
    lasts = [t_second(d, e) for d in range(nz) for e in range(ncol) if d + e > 0]
    for c in lasts:
        c.start()
    row_sq = rowbuf[0]
    for d in range(1, ncol):
        row_sq = row_sq + rowbuf[d]
    new_row = decay * rm_ref[...].reshape(1, rows) + (1.0 - decay) * row_sq / F
    nr_ref[...] = new_row
    nrc_ref[...] = jnp.transpose(jnp.broadcast_to(new_row, (128, new_row.shape[1])))
    finish(seconds)
    col_sq = colz[0]
    for d in range(1, nz):
        col_sq = col_sq + colz[d]
    nc_ref[...] = decay * cm_ref[...].reshape(1, width) + (1.0 - decay) * col_sq / D
    finish(lasts)
    total = totz[0]
    for k in range(1, nz * ncol):
        total = total + totz[k]
    mt_ref[...] = total

    for h in range(PIECES):
        for zz in range(nz):
            @pl.when((z < nz - 1) & (zz <= z))
            def _():
                to_up(place(slot(o, zz), h), o, zz, h).wait_send()

            @pl.when((z > 0) & (zz >= z))
            def _():
                to_down(place(slot(o, zz), h), o, zz, h).wait_send()

            @pl.when((zz != mate) | (h < BY_Y))
            def _():
                to_y(place(slot(o, zz), h), zz, h).wait_send()

            to_partner(place(slot(o, zz), h), o, zz, h).wait_send()
            to_partner(place(slot(oy, zz), h), oy, zz, h).wait_send()
        if h >= BY_Y:
            extra(h, lambda c: c.wait_send())
    for d in range(1, nout):
        a_first(d).wait_send()
    for oo in range(nout):
        for d in range(1, ncol):
            a_second(oo, d).wait_send()


def update_kernel(step, grad_ref, nr_ref, nc_ref, mt_ref, flat_ref, out_ref, row_ref, col_ref):
    here = pl.ds(pl.multiple_of(pl.program_id(0) * step, step), step)
    scale = D / mt_ref[0, 0]
    by_row = lax.rsqrt(nr_ref[here, :1])
    by_col = lax.rsqrt(nc_ref[...] * scale)
    @pl.when(pl.program_id(0) == 0)
    def _():
        row_ref[...] = flat_ref[...].reshape(row_ref.shape)
        col_ref[...] = nc_ref[...].reshape(col_ref.shape)

    out_ref[...] = (grad_ref[here, :] * by_row * by_col).astype(out_ref.dtype)


def body(nout, nz, ncol, activations, out_grads, row_moment, col_moment):
    rows, width = row_moment.shape[0], col_moment.shape[0]
    ta, tg = activations.shape[0], out_grads.shape[0]
    tokens = ta * ncol * nout
    decay = 1.0 - STEP ** (-0.8)
    f32, bf16 = jnp.float32, jnp.bfloat16
    vmem = pl.BlockSpec(memory_space=pltpu.VMEM)
    dma = pltpu.SemaphoreType.DMA
    grad, new_row, turned_row, new_col, total = pl.pallas_call(
        functools.partial(kernel, nout, nz, ncol, 1.0 / tokens**0.5, decay),
        out_shape=(
            pltpu.VMEM((rows, width), f32),
            jax.ShapeDtypeStruct((1, rows), f32),
            pltpu.VMEM((rows, 128), f32),
            jax.ShapeDtypeStruct((1, width), f32),
            jax.ShapeDtypeStruct((1, 128), f32),
        ),
        in_specs=[pl.BlockSpec(memory_space=pl.ANY)] * 4,
        out_specs=(vmem,) * 5,
        scratch_shapes=[
            pltpu.VMEM((tokens, width), bf16),
            pltpu.VMEM((nout * ncol, rows, ta), bf16),
            pltpu.VMEM(activations.shape, bf16),
            pltpu.VMEM((nout, rows, ta), bf16),
            pltpu.VMEM((rows,), f32),
            pltpu.VMEM((width,), f32),
            pltpu.VMEM((rows, 128), f32),
            pltpu.VMEM((nout, 1, width), f32),
            pltpu.VMEM((nz, 1, width), f32),
            pltpu.VMEM((ncol, 1, rows), f32),
            pltpu.VMEM((nz * ncol, 1, 128), f32),
            pltpu.VMEM((nout, 1, 128), f32),
            dma((nout * nz, PIECES)),
            dma((nz + 1, PIECES)),
            dma((nz + 1, PIECES)),
            dma((nz, PIECES)),
            dma((2 * nz, PIECES)),
            dma((nout * ncol,)),
            dma((nout,)),
            dma((nout, ncol)),
            dma((5,)),
            dma((nout,)), dma((nout,)),
            dma((nz,)), dma((nz,)),
            dma((ncol,)), dma((ncol,)),
            dma((nz * ncol,)), dma((nz * ncol,)),
            dma((nout,)), dma((nout,)),
        ],
        compiler_params=pltpu.CompilerParams(
            collective_id=0, has_side_effects=True, vmem_limit_bytes=44 * 1024 * 1024
        ),
    )(activations, out_grads, row_moment, col_moment)
    parts = next(n for n in (4, 3, 2, 1) if n == 1 or rows % (n * 16) == 0)
    step = rows // parts
    update, flat_row, flat_col = pl.pallas_call(
        functools.partial(update_kernel, step),
        grid=(parts,),
        out_shape=(
            jax.ShapeDtypeStruct((rows, width), bf16),
            jax.ShapeDtypeStruct((rows,), f32),
            jax.ShapeDtypeStruct((width,), f32),
        ),
        in_specs=[vmem] * 5,
        out_specs=(pl.BlockSpec((step, width), lambda i: (i, 0)), vmem, vmem),
        compiler_params=pltpu.CompilerParams(vmem_limit_bytes=24 * 1024 * 1024),
    )(grad, turned_row, new_col, total, new_row)
    return (update, flat_row, flat_col)


def solution(mesh):
    nout, nz, ncol = mesh.shape["outer"], mesh.shape["row"], mesh.shape["col"]
    return jax.shard_map(
        functools.partial(body, nout, nz, ncol),
        mesh=mesh,
        in_specs=(
            P(("outer", "col"), "row"),
            P(("outer", "row"), "col"),
            P(("row", "outer")),
            P("col"),
        ),
        out_specs=(P(("row", "outer"), "col"), P(("row", "outer")), P("col")),
        check_vma=False,
    )
```
